32 devices in a mesh: gz: 4 (over y, x), ba: 8 (over z, core).
Axes of the slice: x: 2, y: 2, z: 4, core: 2. Of those that a mesh axis runs over, the one named last changes fastest.
Arguments:
- embeddings: bfloat16 [128, 8, 16, 64, 128], P(('gz', 'ba')), may hold values from -6 to 6
- tissue: int32 [128], P(('gz', 'ba')), may hold values from 0 to 1, as said below
- counts: int32 [32], P(('gz', 'ba')), may hold values from 1 to 4, 80 in all
Outputs:
- fine_affinity: bfloat16 [128, 26, 8, 16, 128], P(('gz', 'ba'))
- coarse_affinity: bfloat16 [128, 512], P(('gz', 'ba'))
The draws below stay inside these ranges and needn't reach their ends.
Inputs may be any that keep to these rules, and one draw needn't show every extreme that they name: counts[d] is the number of consecutive bricks of the row held by device d in its first slots (devices in gz-major order); the counts sum to 80 and some device holds 4; slots past counts[d] hold data that is not used. Each slot's tissue flag is 0 or 1.
All inputs are finite; a program needn't handle non-finite values.
Results may differ from the reference program's by a relative error of at most 0.0036.
Values may be sent and summed in bfloat16 or wider, within the bound.
No kernel may reach another device: no remote copies, remote signals or barrier semaphores. Data moves between devices by JAX's collectives and lax.ppermute only.
A program may use at most 128 MiB of HBM per device.

```python
import math
import jax
import jax.numpy as jnp
import numpy as np
from jax import lax

C = 64
EX = 128
EY = 16
EZ = 8
RIM = 27
SLOTS = 4
CO_NEAR = 10
CO_FAR = 30
BRICKS = 80
TOTAL_SLOTS = 128
DEVICES = 32


def draw_tissue(key, part):
    rolls = jax.random.randint(key, (TOTAL_SLOTS,), 0, 4)
    flags = jnp.where(rolls > 0, 1, 0)
    slot_ids = jnp.arange(TOTAL_SLOTS, dtype=jnp.int32)
    forced = (slot_ids >= (DEVICES - 3) * SLOTS) & (slot_ids <= (DEVICES - 1) * SLOTS)
    return jnp.where(forced, 1, flags).astype(jnp.int32)


def level_of(key, dims, split, smallest, top_value):
    def one(position, blocks):
        draws = jax.random.uniform(jax.random.fold_in(jax.random.fold_in(key, 6), position), (blocks,), jnp.float32, smallest / len(split), top_value / len(split))
        return jnp.repeat(jnp.exp(draws), dims[position] // blocks).reshape((-1,) + (1,) * (len(dims) - position - 1))

    level = one(*split[0])
    for cut in split[1:]:
        level = level * one(*cut)
    return level


def split_up(number_of, total, most, skew):
    weights = [(1 << 20) // math.isqrt(standing ** skew) + 1 for standing in range(2, number_of + 1)]
    spare, given = total - most - (number_of - 1), [1] * (number_of - 1)
    while spare > 0:
        candidates = [i for i in range(number_of - 1) if given[i] < most]
        whole, left = sum([weights[i] for i in candidates]), spare
        for i in candidates:
            addition = min(most - given[i], max(1, left * weights[i] // whole), spare)
            given[i] = given[i] + addition
            spare = spare - addition
    return np.array([most] + given)


def ragged(own_key, amount, total, bound, slope):
    if amount == 2:
        one = jax.random.randint(own_key, (), max(1, total - bound), min(bound, total - 1) + 1)
        return jnp.stack([one, total - one])
    sizes = jnp.asarray(split_up(amount, total, bound, slope), jnp.int32)
    pairs = (amount - 1) // 2
    giver, receiver = sizes[1:1 + 2 * pairs:2], sizes[2:2 + 2 * pairs:2]
    room = jnp.minimum(giver - 1, bound - receiver)
    shifted = jax.random.randint(jax.random.fold_in(own_key, 1), (pairs,), 0, 1 << 20) % (room + 1)
    sizes = sizes.at[1:1 + 2 * pairs:2].set(giver - shifted).at[2:2 + 2 * pairs:2].set(receiver + shifted)
    return sizes[jax.random.permutation(jax.random.fold_in(own_key, 2), amount)]


def normal_values(stream_key, extent, scale, reach, split=(), held_as=jnp.bfloat16):
    array = jax.random.normal(stream_key, extent, jnp.float32) * scale
    if len(split) > 0:
        array = level_of(stream_key, extent, split, -0.22, 0.18) * array
    return jnp.clip(array, min=-reach, max=reach).astype(held_as)


def setup_inputs(seed: int = 0) -> dict:
    key_list = jax.random.split(jax.random.key(seed), 4)
    return {
        "embeddings": normal_values(key_list[0], (TOTAL_SLOTS, EZ, EY, C, EX), 1.0, 6.0, ((0, 32),)),
        "tissue": draw_tissue(jax.random.fold_in(key_list[3], 71), 0),
        "counts": ragged(key_list[2], DEVICES, BRICKS, SLOTS, 2).astype(jnp.int32),
    }


FINE_OFFSETS = ((0, 0, 1), (0, 0, 3), (0, 0, 9), (0, 0, 27), (0, 1, 0), (0, 3, 0), (0, 9, 0), (1, 0, 0), (2, 0, 0), (4, 0, 0), (0, 1, 1), (0, 3, 3), (0, 9, 9), (0, 9, 27), (0, -1, 1), (0, -3, 3), (0, -9, 9), (0, -9, 27), (1, 0, 3), (2, 0, 9), (4, 0, 27), (1, 1, 0), (2, 3, 0), (4, 9, 0), (1, 1, 1), (2, 3, 9))
pad_depth = 4
pad_height = 9

def correlate(extended, tissue_own, tissue_left):
    depth, height, channels, span = extended.shape
    width = span - RIM
    padded = jnp.pad(extended, ((pad_depth, 0), (pad_height, pad_height), (0, 0), (0, 0)))
    centre = extended[:, :, :, RIM:].astype(jnp.float32)
    z_index = lax.broadcasted_iota(jnp.int32, (depth, height, width), 0)
    y_index = lax.broadcasted_iota(jnp.int32, (depth, height, width), 1)
    x_index = lax.broadcasted_iota(jnp.int32, (depth, height, width), 2)
    factor = 1.0 / math.sqrt(channels)
    results = []
    for step_z, step_y, step_x in FINE_OFFSETS:
        partner = padded[pad_depth - step_z:pad_depth - step_z + depth, pad_height - step_y:pad_height - step_y + height, :, RIM - step_x:RIM - step_x + width].astype(jnp.float32)
        score = jnp.einsum('zycx,zycx->zyx', centre, partner)
        inside = (z_index >= step_z) & (y_index >= step_y) & (y_index - step_y < height)
        partner_tissue = jnp.where(x_index >= step_x, tissue_own, tissue_left)
        weight = jnp.where(inside, partner_tissue * tissue_own, 0.0)
        results.append(jax.nn.sigmoid(score * factor) * weight)
    return jnp.stack(results).astype(jnp.bfloat16)

def pool_brick(brick):
    depth, height, channels, width = brick.shape
    blocks = brick.astype(jnp.float32).reshape(depth, height // 8, 8, channels, width // 8, 8)
    average = lax.optimization_barrier(jnp.sum(blocks, axis=(2, 5))) / 64.0
    scale = lax.rsqrt(lax.optimization_barrier(jnp.mean(average * average, axis=2, keepdims=True)) + 1e-06)
    return (average * scale).astype(jnp.bfloat16)

def coarse_brick(row_block, mark_row):
    cells_x = row_block.shape[-1] // 3
    centre = row_block[..., 2 * cells_x:].astype(jnp.float32)
    factor = 1.0 / math.sqrt(row_block.shape[2])
    results = []
    for offset in (CO_NEAR, CO_FAR):
        partner = row_block[..., 2 * cells_x - offset:3 * cells_x - offset].astype(jnp.float32)
        score = jnp.einsum('zycx,zycx->zyx', centre, partner)
        weight = mark_row[2 * cells_x:] * mark_row[2 * cells_x - offset:3 * cells_x - offset]
        results.append(jax.nn.sigmoid(score * factor) * weight)
    return jnp.stack(results).reshape(-1)

def reference(embeddings, tissue, counts):
    slot_ids = jnp.arange(TOTAL_SLOTS, dtype=jnp.int32)
    owner = slot_ids // SLOTS
    within = slot_ids % SLOTS
    starts = (jnp.cumsum(counts) - counts).astype(jnp.int32)
    live = within < counts[owner]
    brick_of_slot = jnp.where(live, starts[owner] + within, BRICKS).astype(jnp.int32)
    order = jnp.zeros((BRICKS + 1,), jnp.int32).at[brick_of_slot].set(slot_ids)
    tissue_float = tissue.astype(jnp.float32)
    previous = order[jnp.maximum(brick_of_slot - 1, 0).astype(jnp.int32)]
    previous_tissue = jnp.where(brick_of_slot >= 1, tissue_float[previous], 0.0)

    def fine_slot(entry):
        index, left_index, left_tissue, active = entry
        brick = embeddings[index]
        left_rim = embeddings[left_index][:, :, :, EX - RIM:]
        result = correlate(jnp.concatenate([left_rim, brick], -1), tissue_float[index], left_tissue)
        return jnp.where(active, result, jnp.zeros_like(result))
    fine_affinity = lax.map(fine_slot, (slot_ids, previous, previous_tissue, live))
    pooled = lax.map(pool_brick, embeddings)

    def earlier(back):
        valid = brick_of_slot >= back
        source = order[jnp.clip(brick_of_slot - back, 0, BRICKS).astype(jnp.int32)]
        cell_rows = jnp.where(valid[:, None, None, None, None], pooled[source], jnp.zeros_like(pooled))
        flag_rows = jnp.where(valid, tissue_float[source], 0.0)
        return (cell_rows, flag_rows)
    far_cells, far_flags = earlier(2)
    near_cells, near_flags = earlier(1)
    row_blocks = jnp.concatenate([far_cells, near_cells, pooled], -1)
    cells_x = pooled.shape[-1]
    mark_rows = jnp.concatenate([jnp.repeat(far_flags[:, None], cells_x, 1), jnp.repeat(near_flags[:, None], cells_x, 1), jnp.repeat(tissue_float[:, None], cells_x, 1)], 1)
    coarse = jax.vmap(coarse_brick)(row_blocks, mark_rows)
    coarse_affinity = jnp.where(live[:, None], coarse, 0.0).astype(jnp.bfloat16)
    return (fine_affinity, coarse_affinity)
```

```python
import functools
import math

import jax
import jax.numpy as jnp
from jax import lax
from jax.experimental import pallas as pl
from jax.experimental.pallas import tpu as pltpu
from jax.sharding import PartitionSpec as P

CO_NEAR = 10
CO_FAR = 30
POOL = 8
PACK = 32

FINE_OFFSETS = (
    (0, 0, 1),
    (0, 0, 3),
    (0, 0, 9),
    (0, 0, 27),
    (0, 1, 0),
    (0, 3, 0),
    (0, 9, 0),
    (1, 0, 0),
    (2, 0, 0),
    (4, 0, 0),
    (0, 1, 1),
    (0, 3, 3),
    (0, 9, 9),
    (0, 9, 27),
    (0, -1, 1),
    (0, -3, 3),
    (0, -9, 9),
    (0, -9, 27),
    (1, 0, 3),
    (2, 0, 9),
    (4, 0, 27),
    (1, 1, 0),
    (2, 3, 0),
    (4, 9, 0),
    (1, 1, 1),
    (2, 3, 9),
)
SHIFTS = (1, 3, 9, 27)
STEPS_Y = (0, 1, 3, 9, -1, -3, -9)
STEPS_Z = (1, 2, 4)
RIM_TURNS = ((1, 0), (3, 0), (9, 0), (27, 0), (3, 1), (1, 1), (9, 2))


def iota(shape, dim):
    return lax.broadcasted_iota(jnp.int32, shape, dim)


def y_range(step, height):
    return max(0, step), min(height, height + step)


def sum_pattern(step, height, rows, scale):
    first, last = y_range(step, height)
    shape = (height, (last - first) * rows)
    hit = iota(shape, 1) // rows + first == iota(shape, 0)
    return jnp.where(hit, scale, 0.0).astype(jnp.bfloat16)


def write_patterns(ref, height, rows, channels):
    for k, step in enumerate(STEPS_Y):
        pattern = sum_pattern(step, height, rows, 0.5 / math.sqrt(channels))
        ref[k, :, : pattern.shape[1]] = pattern


def half_product(left, right):
    product = left * right
    half = product.shape[0] // 2
    return product[:half] + product[half:]


def affinity_of(step_y, height, patterns, centre, partner):
    first, last = y_range(step_y, height)
    products = jnp.concatenate(
        [half_product(centre(y), partner(y - step_y)) for y in range(first, last)], 0
    )
    pattern = patterns[STEPS_Y.index(step_y), :, : products.shape[0]]
    score = jnp.dot(pattern, products, preferred_element_type=jnp.float32)
    return 0.5 * jnp.tanh(score) + 0.5


def pool_pattern(lane0, width):
    k, lane = iota((width, width), 0), iota((width, width), 1)
    hit = k // POOL + lane0 == lane
    return jnp.where(hit, 1.0 / (POOL * POOL), 0.0).astype(jnp.bfloat16)


def pooled_cells(rows, pattern):
    average = jnp.dot(rows[0], pattern, preferred_element_type=jnp.float32)
    for row in rows[1:]:
        average = average + jnp.dot(row, pattern, preferred_element_type=jnp.float32)
    mean = jnp.mean(average * average, axis=0, keepdims=True)
    return average * lax.rsqrt(mean + 1e-6)


def pack_rows(read, first_z, y, turn, lanes):
    group = lanes // PACK
    result = None
    for j in range(lanes.shape[1] // PACK):
        value = read(first_z + j, y)
        shift = (PACK * j + turn) % lanes.shape[1]
        if shift:
            value = pltpu.roll(value, shift, 1)
        result = value if result is None else jnp.where(group == j, value, result)
    return result


def send_kernel(counts, tissue, embeddings, send_ref, far_ref, bricks, sems):
    _, depth, height, channels, width = bricks.shape
    count = counts[0]
    last = count - 1
    second = jnp.maximum(count - 2, 0)
    copies = []
    for k, slot in enumerate((last, second)):
        for z in range(depth):
            copy = pltpu.make_async_copy(embeddings.at[slot, z], bricks.at[k, z], sems.at[k, z])
            copy.start()
            copies.append(copy)
    lanes = iota((channels, width), 1)
    zs = width // PACK
    read = lambda z, y: bricks[0, z, y]
    for group in range(depth // zs):
        for z in range(group * zs, group * zs + zs):
            copies[z].wait()
        for y in range(height):
            packed = pack_rows(read, group * zs, y, PACK, lanes)
            row = (group * height + y) * channels
            send_ref[row : row + channels, :] = packed
    rim_rows = depth // zs * height * channels
    for z in range(depth):
        copies[depth + z].wait()
    cells = width // POOL
    tiles = depth * height // POOL
    per_row = width // (2 * cells)
    for block in range(tiles // per_row):
        total = jnp.zeros((channels, width), jnp.float32)
        for part in range(per_row):
            tile = block * per_row + part
            z, y0 = tile // (height // POOL), tile % (height // POOL) * POOL
            for k in range(2):
                pattern = pool_pattern((2 * part + 1 - k) * cells, width)
                total += pooled_cells([bricks[k, z, y0 + i] for i in range(POOL)], pattern)
        total = total.astype(jnp.bfloat16)
        send_ref[rim_rows + block * channels : rim_rows + (block + 1) * channels, :] = total
        far_ref[block * channels : (block + 1) * channels, :] = total
    own_mark = tissue[last].astype(jnp.float32)
    has_two = (count >= 2).astype(jnp.float32)
    second_mark = tissue[second].astype(jnp.float32) * has_two
    row = iota((16, width), 0)
    flags = jnp.where(row == 0, own_mark, jnp.where(row == 1, second_mark, has_two))
    flags = flags.astype(jnp.bfloat16)
    pool_rows = tiles // per_row * channels
    send_ref[rim_rows + pool_rows :, :] = flags
    far_ref[pool_rows:, :] = flags


def fine_kernel(
    counts, tissue, embeddings, fine_ref, pooled_ref, head_ref, bricks, shifted, patterns, sems
):
    slots, depth, height, channels, width = bricks.shape
    slot = pl.program_id(0)

    def running(k):
        return (k < counts[0]) & (tissue[k] > 0)

    def plane_copy(k, z):
        return pltpu.make_async_copy(embeddings.at[k, z], bricks.at[k, z], sems.at[k, z])

    @pl.when(slot == 0)
    def _():
        for k in range(slots):

            @pl.when(running(k))
            def _():
                for z in range(depth):
                    plane_copy(k, z).start()

        write_patterns(patterns, height, channels // 2, channels)
        pooled_ref[...] = jnp.zeros_like(pooled_ref)
        head_ref[...] = jnp.zeros_like(head_ref)

    active = running(slot)
    before = jnp.maximum(slot - 1, 0)
    left_ok = (slot > 0) & (tissue[before] > 0)
    lanes = iota((channels, width), 1)
    out_y, out_x = iota((height, width), 0), iota((height, width), 1)
    cells = width // POOL

    @pl.when(jnp.logical_not(active))
    def _():
        fine_ref[...] = jnp.zeros_like(fine_ref)

    @pl.when(active)
    def _():
        def plane(z, carry):
            plane_copy(slot, z).wait()
            for y in range(height):
                own, prior = bricks[slot, z, y], bricks[before, z, y]
                for k, step in enumerate(SHIFTS):
                    joined = jnp.where(lanes >= width - step, prior, own)
                    shifted[k, z, y] = pltpu.roll(joined, step, 1)
            pattern = pool_pattern((slot + 2) * cells, width)
            for half in range(height // POOL):
                rows = [bricks[slot, z, half * POOL + i] for i in range(POOL)]
                value = pooled_cells(rows, pattern).astype(jnp.bfloat16)
                row = pl.multiple_of((z * (height // POOL) + half) * channels, channels)
                place = pl.ds(row, channels)
                pooled_ref[place, :] = jnp.where(
                    lanes // cells == slot + 2, value, pooled_ref[place, :]
                )

            def affinity(index):
                step_z, step_y, step_x = FINE_OFFSETS[index]
                centre = lambda y: bricks[slot, z, y]
                if step_x:
                    partner = lambda y: shifted[SHIFTS.index(step_x), z - step_z, y]
                else:
                    partner = lambda y: bricks[slot, z - step_z, y]
                value = affinity_of(step_y, height, patterns, centre, partner)
                first, last = y_range(step_y, height)
                inside = None
                if step_x:
                    inside = out_x >= jnp.where(left_ok, 0, step_x)
                if first > 0:
                    test = out_y >= first
                    inside = test if inside is None else inside & test
                if last < height:
                    test = out_y < last
                    inside = test if inside is None else inside & test
                if inside is not None:
                    value = jnp.where(inside, value, 0.0)
                fine_ref[0, index, z] = value.astype(jnp.bfloat16)

            for index, offset in enumerate(FINE_OFFSETS):
                if offset[0] == 0:
                    affinity(index)
            for step_z in STEPS_Z:
                members = [i for i, offset in enumerate(FINE_OFFSETS) if offset[0] == step_z]

                @pl.when(z >= step_z)
                def _():
                    for index in members:
                        affinity(index)

                @pl.when(z < step_z)
                def _():
                    for index in members:
                        fine_ref[0, index, z] = jnp.zeros((height, width), jnp.bfloat16)

            return carry

        lax.fori_loop(0, depth, plane, 0)

    @pl.when(active & (slot == 0))
    def _():
        zs = width // PACK
        read = lambda z, y: bricks[0, z, y]
        for group in range(depth // zs):
            for y in range(height):
                row = (group * height + y) * channels
                head_ref[row : row + channels, :] = pack_rows(read, group * zs, y, 0, lanes)


def join_kernel(
    counts,
    tissue,
    near_ref,
    far_ref,
    pooled_ref,
    head_ref,
    fine_in,
    fine_out,
    coarse_ref,
    fine,
    turned,
    patterns,
    sems,
):
    slots, cells_total = coarse_ref.shape
    _, depth, height, width = fine.shape
    channels = turned.shape[3]
    zs = width // PACK
    groups = depth // zs
    cells = width // POOL
    tiles = depth * height // POOL
    per_row = width // (2 * cells)
    rim_rows = groups * height * channels
    pool_rows = tiles // per_row * channels
    active = tissue[0] > 0
    fetch = pltpu.make_async_copy(fine_in.at[0], fine, sems.at[0])
    store = pltpu.make_async_copy(fine, fine_out.at[0], sems.at[1])

    @pl.when(active)
    def _():
        fetch.start()

    lanes = iota((channels, width), 1)
    near_flags = near_ref[rim_rows + pool_rows :, :].astype(jnp.float32)
    far_flags = far_ref[pool_rows:, :].astype(jnp.float32)
    near_mark, second_mark, has_two = near_flags[0:1], near_flags[1:2], near_flags[2:3]
    far_mark = jnp.where(has_two > 0, second_mark, far_flags[0:1])

    out_x = iota((1, width), 1)
    mark = jnp.where(out_x < cells, far_mark, near_mark)
    for k in range(slots):
        own = jnp.where((k < counts[0]) & (tissue[k] > 0), 1.0, 0.0)
        mark = jnp.where(out_x >= (k + 2) * cells, own, mark)
    mark = jnp.where(out_x >= (slots + 2) * cells, 0.0, mark)
    offsets = (CO_NEAR, CO_FAR)
    scores = [[] for _ in offsets]
    for tile in range(tiles):
        block, part = tile // per_row, tile % per_row
        rows = slice(rim_rows + block * channels, rim_rows + (block + 1) * channels)
        far_rows = slice(block * channels, (block + 1) * channels)
        near = pltpu.roll(near_ref[rows, :].astype(jnp.float32), width - 2 * part * cells, 1) if part else near_ref[rows, :].astype(jnp.float32)
        far = pltpu.roll(far_ref[far_rows, :].astype(jnp.float32), width - (2 * part + 1) * cells, 1)
        far = jnp.where((has_two <= 0) & (lanes < cells), far, near)
        own = pooled_ref[tile * channels : (tile + 1) * channels, :].astype(jnp.float32)
        row = jnp.where(lanes < 2 * cells, far, own)
        for k, offset in enumerate(offsets):
            scores[k].append(jnp.sum(row * pltpu.roll(row, offset, 1), axis=0, keepdims=True))
    tables = []
    for k, offset in enumerate(offsets):
        score = jnp.concatenate(scores[k], 0)
        weight = mark * pltpu.roll(mark, offset, 1)
        value = 0.5 * jnp.tanh(score * (0.5 / math.sqrt(channels))) + 0.5
        tables.append(value * weight)
    table = jnp.concatenate(tables, 0).astype(jnp.bfloat16)
    count = table.shape[0]
    source, target = iota((width, cells_total), 0), iota((width, cells_total), 1)
    chosen = iota((count, cells_total), 0) == iota((count, cells_total), 1) // cells
    for k in range(slots):
        pick = jnp.where(source == (k + 2) * cells + target % cells, 1.0, 0.0).astype(jnp.bfloat16)
        spread = jnp.dot(table, pick, preferred_element_type=jnp.float32)
        line = jnp.sum(jnp.where(chosen, spread, 0.0), axis=0, keepdims=True)
        coarse_ref[k : k + 1, :] = line.astype(jnp.bfloat16)

    @pl.when(active)
    def _():
        write_patterns(patterns, height, channels // 2, channels)

        def rim(group, y):
            row = (group * height + y) * channels
            return near_ref[row : row + channels, :]

        def head(group, y):
            row = (group * height + y) * channels
            return head_ref[row : row + channels, :]

        for k, (step_x, step_z) in enumerate(RIM_TURNS):
            shift = (step_x + PACK * step_z - PACK) % width
            for y in range(height):
                held = None
                for group in range(groups):
                    value = pltpu.roll(rim(group, y), shift, 1)
                    fresh = value
                    if held is not None and step_z:
                        fresh = jnp.where(lanes < PACK * step_z, held, value)
                    turned[k, group, y] = fresh
                    held = value
        fetch.wait()
        in_y, in_x = iota((height, width), 0), iota((height, width), 1)
        near_rows = jnp.broadcast_to(near_mark, (height, width))
        for index, (step_z, step_y, step_x) in enumerate(FINE_OFFSETS):
            if step_x == 0:
                continue
            for group in range(groups):
                if (group + 1) * zs <= step_z:
                    continue
                if step_z >= zs:
                    turn, source_group = RIM_TURNS.index((step_x, 0)), group - step_z // zs
                else:
                    turn, source_group = RIM_TURNS.index((step_x, step_z)), group
                value = affinity_of(
                    step_y,
                    height,
                    patterns,
                    lambda y: head(group, y),
                    lambda y: turned[turn, source_group, y],
                )
                first, last = y_range(step_y, height)
                inside = near_rows > 0
                if first > 0:
                    inside = inside & (in_y >= first)
                if last < height:
                    inside = inside & (in_y < last)
                value = jnp.where(inside, value, 0.0)
                for j in range(zs):
                    z = group * zs + j
                    if z < step_z:
                        continue
                    moved = pltpu.roll(value, (width - PACK * j) % width, 1) if j else value
                    old = fine[index, z]
                    fine[index, z] = jnp.where(in_x < step_x, moved.astype(jnp.bfloat16), old)
        store.start()
        store.wait()


def body(embeddings, tissue, counts):
    slots, depth, height, channels, width = embeddings.shape
    offsets = len(FINE_OFFSETS)
    cells = width // POOL
    tiles = depth * height // POOL
    groups = depth // (width // PACK)
    rim_rows = groups * height * channels
    pool_rows = tiles * 2 * cells // width * channels
    smem = pl.BlockSpec(memory_space=pltpu.SMEM)
    anyspace = pl.BlockSpec(memory_space=pl.ANY)
    vmem = pl.BlockSpec(memory_space=pltpu.VMEM)
    half = jnp.bfloat16
    big = 60 * 1024 * 1024

    send, far = pl.pallas_call(
        send_kernel,
        out_shape=(
            jax.ShapeDtypeStruct((rim_rows + pool_rows + 16, width), half),
            jax.ShapeDtypeStruct((pool_rows + 16, width), half),
        ),
        in_specs=[smem, smem, anyspace],
        out_specs=(vmem, vmem),
        scratch_shapes=[
            pltpu.VMEM((2, depth, height, channels, width), half),
            pltpu.SemaphoreType.DMA((2, depth)),
        ],
        compiler_params=pltpu.CompilerParams(vmem_limit_bytes=big),
        name="send",
    )(counts, tissue, embeddings)

    axes = ("gz", "ba")
    devices = lax.axis_size(axes)
    near_in = lax.ppermute(send, axes, [(d, d + 1) for d in range(devices - 1)])
    far_in = lax.ppermute(far, axes, [(d, d + 2) for d in range(devices - 2)])

    fine, pooled, head = pl.pallas_call(
        fine_kernel,
        grid_spec=pltpu.PrefetchScalarGridSpec(
            num_scalar_prefetch=2,
            grid=(slots,),
            in_specs=[anyspace],
            out_specs=(
                pl.BlockSpec((1, offsets, depth, height, width), lambda s, *_: (s, 0, 0, 0, 0)),
                pl.BlockSpec((tiles * channels, width), lambda s, *_: (0, 0)),
                pl.BlockSpec((rim_rows, width), lambda s, *_: (0, 0)),
            ),
            scratch_shapes=[
                pltpu.VMEM((slots, depth, height, channels, width), half),
                pltpu.VMEM((len(SHIFTS), depth, height, channels, width), half),
                pltpu.VMEM((len(STEPS_Y), height, height * channels // 2), half),
                pltpu.SemaphoreType.DMA((slots, depth)),
            ],
        ),
        out_shape=(
            jax.ShapeDtypeStruct((slots, offsets, depth, height, width), half),
            jax.ShapeDtypeStruct((tiles * channels, width), half),
            jax.ShapeDtypeStruct((rim_rows, width), half),
        ),
        compiler_params=pltpu.CompilerParams(vmem_limit_bytes=big),
        cost_estimate=pl.CostEstimate(
            flops=20_000_000_000, bytes_accessed=20_000_000, transcendentals=0
        ),
        name="fine",
    )(counts, tissue, embeddings)

    return pl.pallas_call(
        join_kernel,
        out_shape=(
            jax.ShapeDtypeStruct(fine.shape, half),
            jax.ShapeDtypeStruct((slots, 2 * tiles * cells), half),
        ),
        in_specs=[smem, smem, vmem, vmem, vmem, vmem, anyspace],
        out_specs=(anyspace, vmem),
        scratch_shapes=[
            pltpu.VMEM((offsets, depth, height, width), half),
            pltpu.VMEM((len(RIM_TURNS), groups, height, channels, width), half),
            pltpu.VMEM((len(STEPS_Y), height, height * channels // 2), half),
            pltpu.SemaphoreType.DMA((2,)),
        ],
        input_output_aliases={6: 0},
        compiler_params=pltpu.CompilerParams(vmem_limit_bytes=big),
        name="join",
    )(counts, tissue, near_in, far_in, pooled, head, fine)


def solution(mesh):
    in_specs = (P(("gz", "ba"), None, None, None, None), P(("gz", "ba")), P(("gz", "ba")))
    out_specs = (P(("gz", "ba"), None, None, None, None), P(("gz", "ba"), None))
    return jax.shard_map(body, mesh=mesh, in_specs=in_specs, out_specs=out_specs, check_vma=False)
```

```python
import math

import jax
import jax.numpy as jnp
from jax import lax
from jax.experimental import pallas as pl
from jax.experimental.pallas import tpu as pltpu
from jax.sharding import PartitionSpec as P

CO_NEAR = 10
CO_FAR = 30
POOL = 8
PACK = 32

FINE_OFFSETS = (
    (0, 0, 1),
    (0, 0, 3),
    (0, 0, 9),
    (0, 0, 27),
    (0, 1, 0),
    (0, 3, 0),
    (0, 9, 0),
    (1, 0, 0),
    (2, 0, 0),
    (4, 0, 0),
    (0, 1, 1),
    (0, 3, 3),
    (0, 9, 9),
    (0, 9, 27),
    (0, -1, 1),
    (0, -3, 3),
    (0, -9, 9),
    (0, -9, 27),
    (1, 0, 3),
    (2, 0, 9),
    (4, 0, 27),
    (1, 1, 0),
    (2, 3, 0),
    (4, 9, 0),
    (1, 1, 1),
    (2, 3, 9),
)
SHIFTS = (1, 3, 9, 27)
STARTS = (0, 1, 3)
RIM_TURNS = ((1, 0), (3, 0), (9, 0), (27, 0), (3, 1), (1, 1), (9, 2))


def iota(shape, dim):
    return lax.broadcasted_iota(jnp.int32, shape, dim)


def write_patterns(ref, channels):
    _, rows, width = ref.shape
    scale = 0.5 / math.sqrt(channels)
    for k, start in enumerate(STARTS):
        hit = iota((rows, width), 1) // (channels // 2) + start == iota((rows, width), 0)
        ref[k] = jnp.where(hit, scale, 0.0).astype(jnp.bfloat16)


def half_product(left, right):
    product = left * right
    half = product.shape[0] // 2
    return product[:half] + product[half:]


def valid_rows(step_y, height, first):
    start = max(first, step_y, 0)
    stop = min(first + POOL, height + min(step_y, 0))
    return start, stop


def affinity_of(step_y, height, first, patterns, centre, partner):
    start, stop = valid_rows(step_y, height, first)
    products = [half_product(centre(y), partner(y - step_y)) for y in range(start, stop)]
    products = jnp.concatenate(products, 0)
    pattern = patterns[STARTS.index(start - first), :, : products.shape[0]]
    score = jnp.dot(pattern, products, preferred_element_type=jnp.float32)
    return 0.5 * jnp.tanh(score) + 0.5


def row_test(step_y, height, first, rows):
    start, stop = valid_rows(step_y, height, first)
    test = None
    if start > first:
        test = rows >= start - first
    if stop < first + POOL:
        upper = rows < stop - first
        test = upper if test is None else test & upper
    return test


def both(left, right):
    if left is None or right is None:
        return left if right is None else right
    return left & right


def pool_pattern(width):
    k, lane = iota((width, width), 0), iota((width, width), 1)
    hit = k // POOL == lane % (width // POOL)
    return jnp.where(hit, 1.0 / (POOL * POOL), 0.0).astype(jnp.bfloat16)


def pooled_cells(rows, pattern):
    joined = jnp.concatenate(rows, 1)
    spread = jnp.concatenate([pattern] * len(rows), 0)
    average = jnp.dot(joined, spread, preferred_element_type=jnp.float32)
    mean = jnp.mean(average * average, axis=0, keepdims=True)
    return average * lax.rsqrt(mean + 1e-6)


def pack_rows(values, turn, lanes):
    group = lanes // PACK
    width = lanes.shape[1]
    result = None
    for j, value in enumerate(values):
        shift = (PACK * j + turn) % width
        if shift:
            value = pltpu.roll(value, shift, 1)
        result = value if result is None else jnp.where(group == j, value, result)
    return result


def send_kernel(counts, tissue, embeddings, send_ref, far_ref):
    _, depth, height, channels, width = embeddings.shape
    cells = width // POOL
    tiles = depth * height // POOL
    per_row = width // (2 * cells)
    zs = width // PACK
    rim_rows = depth // zs * height * channels
    pool_rows = tiles // per_row * channels

    def run(bricks, send, sems):
        count = counts[0]
        last = count - 1
        second = jnp.maximum(count - 2, 0)
        copies = {}
        for z in range(depth):
            for k, slot in enumerate((last, second)):
                copy = pltpu.make_async_copy(embeddings.at[slot, z], bricks.at[k, z], sems.at[k, z])
                copy.start()
                copies[k, z] = copy
        lanes = iota((channels, width), 1)
        pattern = pool_pattern(width)
        own_mark = tissue[last].astype(jnp.float32)
        has_two = (count >= 2).astype(jnp.float32)
        second_mark = tissue[second].astype(jnp.float32) * has_two
        row = iota((16, width), 0)
        flags = jnp.where(row == 0, own_mark, jnp.where(row == 1, second_mark, has_two))
        send[rim_rows + pool_rows :, :] = flags.astype(jnp.bfloat16)
        planes = per_row * POOL // height
        for group in range(depth // zs):
            for z in range(group * zs, group * zs + zs):
                copies[0, z].wait()
                copies[1, z].wait()
            for y in range(height):
                values = [bricks[0, group * zs + j, y] for j in range(zs)]
                place = (group * height + y) * channels
                send[place : place + channels, :] = pack_rows(values, PACK, lanes)
            for block in range(group * zs // planes, (group + 1) * zs // planes):
                total = jnp.zeros((channels, width), jnp.float32)
                for part in range(per_row):
                    tile = block * per_row + part
                    z, y0 = tile // (height // POOL), tile % (height // POOL) * POOL
                    for k in range(2):
                        rows = [bricks[k, z, y0 + i] for i in range(POOL)]
                        value = pooled_cells(rows, pattern)
                        total = jnp.where(lanes // cells == 2 * part + 1 - k, value, total)
                place = rim_rows + block * channels
                send[place : place + channels, :] = total.astype(jnp.bfloat16)
        all_out = pltpu.make_async_copy(send, send_ref, sems.at[0, 0])
        far_out = pltpu.make_async_copy(send.at[rim_rows:], far_ref, sems.at[1, 0])
        all_out.start()
        far_out.start()
        all_out.wait()
        far_out.wait()

    pl.run_scoped(
        run,
        pltpu.VMEM((2, depth, height, channels, width), jnp.bfloat16),
        pltpu.VMEM((rim_rows + pool_rows + 16, width), jnp.bfloat16),
        pltpu.SemaphoreType.DMA((2, depth)),
    )


def fine_kernel(counts, tissue, embeddings, fine_ref, pooled_ref, head_ref):
    slots, depth, height, channels, width = embeddings.shape
    offsets = len(FINE_OFFSETS)
    cells = width // POOL
    tiles = depth * height // POOL
    zs = width // PACK
    bf16 = jnp.bfloat16

    def running(k):
        return (k < counts[0]) & (tissue[k] > 0)

    def run(bricks, shifted, fine, pooled, head, patterns, sems, out_sems):
        def plane_copy(k, z):
            return pltpu.make_async_copy(embeddings.at[k, z], bricks.at[k, z], sems.at[k, z])

        def fine_copy(k):
            return pltpu.make_async_copy(fine.at[k], fine_ref.at[k], out_sems.at[k])

        for k in range(slots):

            @pl.when(running(k))
            def _():
                for z in range(depth):
                    plane_copy(k, z).start()

        for k in range(slots):

            @pl.when(jnp.logical_not(running(k)))
            def _():
                fine[k] = jnp.zeros((offsets, depth, height, width), bf16)
                fine_copy(k).start()

        write_patterns(patterns, channels)
        pooled[...] = jnp.zeros_like(pooled)
        lanes = iota((channels, width), 1)
        rows, columns = iota((POOL, width), 0), iota((POOL, width), 1)

        def do_slot(slot, carry):
            before = jnp.maximum(slot - 1, 0)
            left_ok = (slot > 0) & (tissue[before] > 0)
            free = {step: columns >= jnp.where(left_ok, 0, step) for step in SHIFTS}

            def plane(z, steps):
                plane_copy(slot, z).wait()
                for y in range(height):
                    own, prior = bricks[slot, z, y], bricks[before, z, y]
                    for k, step in enumerate(SHIFTS):
                        joined = jnp.where(lanes >= width - step, prior, own)
                        shifted[k, z, y] = pltpu.roll(joined, step, 1)
                pattern = pool_pattern(width)
                for half in range(height // POOL):
                    first = half * POOL
                    centres = [bricks[slot, z, first + i] for i in range(POOL)]
                    value = pooled_cells(centres, pattern).astype(bf16)
                    place = (z * (height // POOL) + half) * channels
                    place = pl.ds(pl.multiple_of(place, channels), channels)
                    keep = lanes // cells == slot + 2
                    pooled[place, :] = jnp.where(keep, value, pooled[place, :])
                    for index, (step_z, step_y, step_x) in enumerate(FINE_OFFSETS):
                        start, stop = valid_rows(step_y, height, first)
                        target = fine.at[slot, index, z, first : first + POOL]
                        if start >= stop or (step_z and step_z not in steps):
                            target[...] = jnp.zeros((POOL, width), bf16)
                            continue
                        centre = lambda y: centres[y - first]
                        if step_x:
                            k = SHIFTS.index(step_x)
                            partner = lambda y: shifted[k, z - step_z, y]
                        else:
                            partner = lambda y: bricks[slot, z - step_z, y]
                        value = affinity_of(step_y, height, first, patterns, centre, partner)
                        inside = both(free.get(step_x), row_test(step_y, height, first, rows))
                        if inside is not None:
                            value = jnp.where(inside, value, 0.0)
                        target[...] = value.astype(bf16)

            @pl.when(running(slot))
            def _():
                edges = sorted({0, depth} | {offset[0] for offset in FINE_OFFSETS})
                for low, high in zip(edges[:-1], edges[1:]):
                    steps = [offset[0] for offset in FINE_OFFSETS if 0 < offset[0] <= low]

                    def one(z, carry):
                        plane(z, steps)
                        return carry

                    lax.fori_loop(low, high, one, 0)
                fine_copy(slot).start()

            return carry

        lax.fori_loop(0, slots, do_slot, 0)

        @pl.when(running(0))
        def _():
            for group in range(depth // zs):
                for y in range(height):
                    values = [bricks[0, group * zs + j, y] for j in range(zs)]
                    place = (group * height + y) * channels
                    head[place : place + channels, :] = pack_rows(values, 0, lanes)

        pooled_copy = pltpu.make_async_copy(pooled, pooled_ref, out_sems.at[slots])
        head_copy = pltpu.make_async_copy(head, head_ref, out_sems.at[slots + 1])
        pooled_copy.start()
        head_copy.start()
        for k in range(slots):
            fine_copy(k).wait()
        pooled_copy.wait()
        head_copy.wait()

    pl.run_scoped(
        run,
        pltpu.VMEM((slots, depth, height, channels, width), bf16),
        pltpu.VMEM((len(SHIFTS), depth, height, channels, width), bf16),
        pltpu.VMEM((slots, offsets, depth, height, width), bf16),
        pltpu.VMEM((tiles * channels, width), bf16),
        pltpu.VMEM((depth // zs * height * channels, width), bf16),
        pltpu.VMEM((len(STARTS), POOL, POOL * channels // 2), bf16),
        pltpu.SemaphoreType.DMA((slots, depth)),
        pltpu.SemaphoreType.DMA((slots + 2,)),
    )


def join_kernel(
    counts, tissue, near_hbm, far_hbm, pooled_hbm, head_hbm, fine_in, fine_out, coarse_ref
):
    slots, cells_total = coarse_ref.shape
    _, offsets_fine, depth, height, width = fine_in.shape
    zs = width // PACK
    groups = depth // zs
    cells = width // POOL
    tiles = depth * height // POOL
    channels = head_hbm.shape[0] // (groups * height)
    per_row = width // (2 * cells)
    rim_rows = groups * height * channels
    pool_rows = tiles // per_row * channels

    def run(near_ref, far_ref, pooled_ref, head_ref, fine, turned, patterns, sems):
        active = tissue[0] > 0
        fetches = [
            pltpu.make_async_copy(source, target, sems.at[k])
            for k, (source, target) in enumerate(
                (
                    (near_hbm, near_ref),
                    (far_hbm, far_ref),
                    (pooled_hbm, pooled_ref),
                    (head_hbm, head_ref),
                    (fine_in.at[0], fine),
                )
            )
        ]
        store = pltpu.make_async_copy(fine, fine_out.at[0], sems.at[5])
        for fetch in fetches:
            fetch.start()
        lanes = iota((channels, width), 1)
        write_patterns(patterns, channels)
        fetches[0].wait()
        fetches[1].wait()
        near_flags = near_ref[rim_rows + pool_rows :, :].astype(jnp.float32)
        far_flags = far_ref[pool_rows:, :].astype(jnp.float32)
        near_mark, second_mark, has_two = near_flags[0:1], near_flags[1:2], near_flags[2:3]
        far_mark = jnp.where(has_two > 0, second_mark, far_flags[0:1])

        @pl.when(active)
        def _():
            def rim(group, y):
                row = (group * height + y) * channels
                return near_ref[row : row + channels, :]

            def head(group, y):
                row = (group * height + y) * channels
                return head_ref[row : row + channels, :]

            for k, (step_x, step_z) in enumerate(RIM_TURNS):
                shift = (step_x + PACK * step_z - PACK) % width
                for y in range(height):
                    held = None
                    for group in range(groups):
                        value = pltpu.roll(rim(group, y), shift, 1)
                        fresh = value
                        if held is not None and step_z:
                            fresh = jnp.where(lanes < PACK * step_z, held, value)
                        turned[k, group, y] = fresh
                        held = value
            fetches[3].wait()
            fetches[4].wait()
            rows, columns = iota((POOL, width), 0), iota((POOL, width), 1)
            near_rows = jnp.broadcast_to(near_mark, (POOL, width)) > 0
            for group in range(groups):
                for first in range(0, height, POOL):
                    centres = [head(group, first + i) for i in range(POOL)]
                    for index, (step_z, step_y, step_x) in enumerate(FINE_OFFSETS):
                        start, stop = valid_rows(step_y, height, first)
                        if step_x == 0 or (group + 1) * zs <= step_z or start >= stop:
                            continue
                        if step_z >= zs:
                            turn, source = RIM_TURNS.index((step_x, 0)), group - step_z // zs
                        else:
                            turn, source = RIM_TURNS.index((step_x, step_z)), group
                        value = affinity_of(
                            step_y,
                            height,
                            first,
                            patterns,
                            lambda y: centres[y - first],
                            lambda y: turned[turn, source, y],
                        )
                        inside = both(near_rows, row_test(step_y, height, first, rows))
                        value = jnp.where(inside, value, 0.0)
                        for j in range(zs):
                            z = group * zs + j
                            if z < step_z:
                                continue
                            moved = value
                            if j:
                                moved = pltpu.roll(value, width - PACK * j, 1)
                            place = fine.at[index, z, first : first + POOL]
                            old = place[...].astype(jnp.float32)
                            fresh = jnp.where(columns < step_x, moved, old)
                            place[...] = fresh.astype(jnp.bfloat16)
            store.start()

        fetches[2].wait()
        out_x = iota((1, width), 1)
        mark = jnp.where(out_x < cells, far_mark, near_mark)
        for k in range(slots):
            own = jnp.where((k < counts[0]) & (tissue[k] > 0), 1.0, 0.0)
            mark = jnp.where(out_x >= (k + 2) * cells, own, mark)
        mark = jnp.where(out_x >= (slots + 2) * cells, 0.0, mark)
        offsets = (CO_NEAR, CO_FAR)
        scores = [[] for _ in offsets]
        for tile in range(tiles):
            block, part = tile // per_row, tile % per_row
            near_rows = slice(rim_rows + block * channels, rim_rows + (block + 1) * channels)
            far_rows = slice(block * channels, (block + 1) * channels)
            near = near_ref[near_rows, :]
            if part:
                near = pltpu.roll(near, width - 2 * part * cells, 1)
            far = pltpu.roll(far_ref[far_rows, :], width - (2 * part + 1) * cells, 1)
            far = jnp.where((has_two <= 0) & (lanes < cells), far.astype(jnp.float32), near.astype(jnp.float32))
            own = pooled_ref[tile * channels : (tile + 1) * channels, :].astype(jnp.float32)
            row = jnp.where(lanes < 2 * cells, far, own)
            for k, offset in enumerate(offsets):
                scores[k].append(jnp.sum(row * pltpu.roll(row, offset, 1), axis=0, keepdims=True))
        tables = []
        for k, offset in enumerate(offsets):
            score = jnp.concatenate(scores[k], 0)
            weight = mark * pltpu.roll(mark, offset, 1)
            value = 0.5 * jnp.tanh(score * (0.5 / math.sqrt(channels))) + 0.5
            tables.append(value * weight)
        table = jnp.concatenate(tables, 0).astype(jnp.bfloat16)
        count = table.shape[0]
        source, target = iota((width, cells_total), 0), iota((width, cells_total), 1)
        chosen = iota((count, cells_total), 0) == iota((count, cells_total), 1) // cells
        for k in range(slots):
            pick = jnp.where(source == (k + 2) * cells + target % cells, 1.0, 0.0)
            spread = jnp.dot(table, pick.astype(jnp.bfloat16), preferred_element_type=jnp.float32)
            line = jnp.sum(jnp.where(chosen, spread, 0.0), axis=0, keepdims=True)
            coarse_ref[k : k + 1, :] = line.astype(jnp.bfloat16)

        @pl.when(active)
        def _():
            store.wait()

        @pl.when(jnp.logical_not(active))
        def _():
            fetches[3].wait()
            fetches[4].wait()

    half = jnp.bfloat16
    pl.run_scoped(
        run,
        pltpu.VMEM(near_hbm.shape, half),
        pltpu.VMEM(far_hbm.shape, half),
        pltpu.VMEM(pooled_hbm.shape, half),
        pltpu.VMEM(head_hbm.shape, half),
        pltpu.VMEM((offsets_fine, depth, height, width), half),
        pltpu.VMEM((len(RIM_TURNS), groups, height, channels, width), half),
        pltpu.VMEM((len(STARTS), POOL, POOL * channels // 2), half),
        pltpu.SemaphoreType.DMA((6,)),
    )


def body(embeddings, tissue, counts):
    slots, depth, height, channels, width = embeddings.shape
    offsets = len(FINE_OFFSETS)
    cells = width // POOL
    tiles = depth * height // POOL
    groups = depth // (width // PACK)
    rim_rows = groups * height * channels
    pool_rows = tiles * 2 * cells // width * channels
    smem = pl.BlockSpec(memory_space=pltpu.SMEM)
    anyspace = pl.BlockSpec(memory_space=pl.ANY)
    vmem = pl.BlockSpec(memory_space=pltpu.VMEM)
    half = jnp.bfloat16
    big = 60 * 1024 * 1024

    send, far = pl.pallas_call(
        send_kernel,
        out_shape=(
            jax.ShapeDtypeStruct((rim_rows + pool_rows + 16, width), half),
            jax.ShapeDtypeStruct((pool_rows + 16, width), half),
        ),
        in_specs=[smem, smem, anyspace],
        out_specs=(anyspace, anyspace),
        compiler_params=pltpu.CompilerParams(vmem_limit_bytes=big),
        name="send",
    )(counts, tissue, embeddings)

    axes = ("gz", "ba")
    devices = lax.axis_size(axes)
    near_in = lax.ppermute(send, axes, [(d, d + 1) for d in range(devices - 1)])
    far_in = lax.ppermute(far, axes, [(d, d + 2) for d in range(devices - 2)])

    fine, pooled, head = pl.pallas_call(
        fine_kernel,
        out_shape=(
            jax.ShapeDtypeStruct((slots, offsets, depth, height, width), half),
            jax.ShapeDtypeStruct((tiles * channels, width), half),
            jax.ShapeDtypeStruct((rim_rows, width), half),
        ),
        in_specs=[smem, smem, anyspace],
        out_specs=(anyspace, anyspace, anyspace),
        compiler_params=pltpu.CompilerParams(vmem_limit_bytes=big),
        cost_estimate=pl.CostEstimate(
            flops=20_000_000_000, bytes_accessed=20_000_000, transcendentals=0
        ),
        name="fine",
    )(counts, tissue, embeddings)

    return pl.pallas_call(
        join_kernel,
        out_shape=(
            jax.ShapeDtypeStruct(fine.shape, half),
            jax.ShapeDtypeStruct((slots, 2 * tiles * cells), half),
        ),
        in_specs=[smem, smem] + [anyspace] * 5,
        out_specs=(anyspace, vmem),
        input_output_aliases={6: 0},
        compiler_params=pltpu.CompilerParams(vmem_limit_bytes=big),
        name="join",
    )(counts, tissue, near_in, far_in, pooled, head, fine)


def solution(mesh):
    in_specs = (P(("gz", "ba"), None, None, None, None), P(("gz", "ba")), P(("gz", "ba")))
    out_specs = (P(("gz", "ba"), None, None, None, None), P(("gz", "ba"), None))
    return jax.shard_map(body, mesh=mesh, in_specs=in_specs, out_specs=out_specs, check_vma=False)
```

```python
import math

import jax
import jax.numpy as jnp
from jax import lax
from jax.experimental import pallas as pl
from jax.experimental.pallas import tpu as pltpu
from jax.sharding import PartitionSpec as P

CO_NEAR = 10
CO_FAR = 30
POOL = 8
PACK = 32

FINE_OFFSETS = (
    (0, 0, 1),
    (0, 0, 3),
    (0, 0, 9),
    (0, 0, 27),
    (0, 1, 0),
    (0, 3, 0),
    (0, 9, 0),
    (1, 0, 0),
    (2, 0, 0),
    (4, 0, 0),
    (0, 1, 1),
    (0, 3, 3),
    (0, 9, 9),
    (0, 9, 27),
    (0, -1, 1),
    (0, -3, 3),
    (0, -9, 9),
    (0, -9, 27),
    (1, 0, 3),
    (2, 0, 9),
    (4, 0, 27),
    (1, 1, 0),
    (2, 3, 0),
    (4, 9, 0),
    (1, 1, 1),
    (2, 3, 9),
)
SHIFTS = (1, 3, 9, 27)
STARTS = (0, 1, 3)
FOLDED = (0, 1, -1, 3, -3, 9, -9)
RIM_TURNS = ((1, 0), (3, 0), (9, 0), (27, 0), (3, 1), (1, 1), (9, 2))


def iota(shape, dim):
    return lax.broadcasted_iota(jnp.int32, shape, dim)


def write_patterns(ref, pair_ref, channels):
    _, rows, width = ref.shape
    scale = 0.5 / math.sqrt(channels)
    for k, start in enumerate(STARTS):
        hit = iota((rows, width), 1) // (channels // 2) + start == iota((rows, width), 0)
        ref[k] = jnp.where(hit, scale, 0.0).astype(jnp.bfloat16)
    row, column = iota((2 * rows, width), 0), iota((2 * rows, width), 1)
    place = column // (channels // 4)
    for i, low in enumerate(STARTS):
        for j, high in enumerate(STARTS):
            start = jnp.where(place < rows, low, high)
            hit = (place % rows + start == row % rows) & (place // rows == row // rows)
            pair_ref[i * len(STARTS) + j] = jnp.where(hit, scale, 0.0).astype(jnp.bfloat16)


def folded_product(left, right, levels):
    product = left * right
    for _ in range(levels):
        half = product.shape[0] // 2
        product = product[:half] + product[half:]
    return product


def valid_rows(step_y, height, first):
    start = max(first, step_y, 0)
    stop = min(first + POOL, height + min(step_y, 0))
    return start, stop


def stacked_products(step_y, height, first, levels, centre, partner):
    start, stop = valid_rows(step_y, height, first)
    products = [folded_product(centre(y), partner(y - step_y), levels) for y in range(start, stop)]
    blank = jnp.zeros_like(products[0])
    return products + [blank] * (POOL - len(products)), STARTS.index(start - first)


def squash(score):
    return 0.5 * jnp.tanh(score) + 0.5


def affinity_of(step_y, height, first, patterns, centre, partner):
    products, start = stacked_products(step_y, height, first, 1, centre, partner)
    products = jnp.concatenate(products, 0)
    return squash(jnp.dot(patterns[start], products, preferred_element_type=jnp.float32))


def two_affinities(step_ys, height, first, patterns, centre, partners):
    products, starts = [], []
    for step_y, partner in zip(step_ys, partners):
        more, start = stacked_products(step_y, height, first, 2, centre, partner)
        products += more
        starts.append(start)
    pattern = patterns[starts[0] * len(STARTS) + starts[1]]
    products = jnp.concatenate(products, 0)
    value = squash(jnp.dot(pattern, products, preferred_element_type=jnp.float32))
    return value[:POOL], value[POOL:]


def row_test(step_y, height, first, rows):
    start, stop = valid_rows(step_y, height, first)
    test = None
    if start > first:
        test = rows >= start - first
    if stop < first + POOL:
        upper = rows < stop - first
        test = upper if test is None else test & upper
    return test


def both(left, right):
    if left is None or right is None:
        return left if right is None else right
    return left & right


def pool_pattern(width):
    k, lane = iota((width, width), 0), iota((width, width), 1)
    hit = k // POOL == lane % (width // POOL)
    return jnp.where(hit, 1.0 / (POOL * POOL), 0.0).astype(jnp.bfloat16)


def pooled_cells(blocks, pattern):
    channels = blocks[0][0].shape[0]
    pairs = [
        jnp.concatenate([rows[i], rows[i + 1]], 1)
        for rows in blocks
        for i in range(0, POOL, 2)
    ]
    spread = jnp.concatenate([pattern, pattern], 0)
    parts = jnp.dot(jnp.concatenate(pairs, 0), spread, preferred_element_type=jnp.float32)
    results = []
    for k in range(len(blocks)):
        average = None
        for i in range(POOL // 2):
            place = (k * (POOL // 2) + i) * channels
            part = parts[place : place + channels]
            average = part if average is None else average + part
        mean = jnp.mean(average * average, axis=0, keepdims=True)
        results.append(average * lax.rsqrt(mean + 1e-6))
    return results


def pack_rows(values, turn, lanes):
    group = lanes // PACK
    width = lanes.shape[1]
    result = None
    for j, value in enumerate(values):
        shift = (PACK * j + turn) % width
        if shift:
            value = pltpu.roll(value, shift, 1)
        result = value if result is None else jnp.where(group == j, value, result)
    return result


def send_kernel(counts, tissue, embeddings, send_ref, far_ref):
    _, depth, height, channels, width = embeddings.shape
    cells = width // POOL
    tiles = depth * height // POOL
    per_row = width // (2 * cells)
    zs = width // PACK
    rim_rows = depth // zs * height * channels
    pool_rows = tiles // per_row * channels

    def run(bricks, send, sems):
        count = counts[0]
        last = count - 1
        second = jnp.maximum(count - 2, 0)
        copies = {}
        for z in range(depth):
            for k, slot in enumerate((last, second)):
                copy = pltpu.make_async_copy(embeddings.at[slot, z], bricks.at[k, z], sems.at[k, z])
                copy.start()
                copies[k, z] = copy
        lanes = iota((channels, width), 1)
        pattern = pool_pattern(width)
        own_mark = tissue[last].astype(jnp.float32)
        has_two = (count >= 2).astype(jnp.float32)
        second_mark = tissue[second].astype(jnp.float32) * has_two
        row = iota((16, width), 0)
        flags = jnp.where(row == 0, own_mark, jnp.where(row == 1, second_mark, has_two))
        send[rim_rows + pool_rows :, :] = flags.astype(jnp.bfloat16)
        planes = per_row * POOL // height
        for group in range(depth // zs):
            for z in range(group * zs, group * zs + zs):
                copies[0, z].wait()
                copies[1, z].wait()
            for y in range(height):
                values = [bricks[0, group * zs + j, y] for j in range(zs)]
                place = (group * height + y) * channels
                send[place : place + channels, :] = pack_rows(values, PACK, lanes)
            for block in range(group * zs // planes, (group + 1) * zs // planes):
                total = jnp.zeros((channels, width), jnp.float32)
                for part in range(per_row):
                    tile = block * per_row + part
                    z, y0 = tile // (height // POOL), tile % (height // POOL) * POOL
                    blocks = [[bricks[k, z, y0 + i] for i in range(POOL)] for k in range(2)]
                    for k, value in enumerate(pooled_cells(blocks, pattern)):
                        total = jnp.where(lanes // cells == 2 * part + 1 - k, value, total)
                place = rim_rows + block * channels
                send[place : place + channels, :] = total.astype(jnp.bfloat16)
        all_out = pltpu.make_async_copy(send, send_ref, sems.at[0, 0])
        far_out = pltpu.make_async_copy(send.at[rim_rows:], far_ref, sems.at[1, 0])
        all_out.start()
        far_out.start()
        all_out.wait()
        far_out.wait()

    pl.run_scoped(
        run,
        pltpu.VMEM((2, depth, height, channels, width), jnp.bfloat16),
        pltpu.VMEM((rim_rows + pool_rows + 16, width), jnp.bfloat16),
        pltpu.SemaphoreType.DMA((2, depth)),
    )


def fine_kernel(counts, tissue, embeddings, fine_ref, pooled_ref, head_ref):
    slots, depth, height, channels, width = embeddings.shape
    offsets = len(FINE_OFFSETS)
    cells = width // POOL
    tiles = depth * height // POOL
    zs = width // PACK
    bf16 = jnp.bfloat16

    def running(k):
        return (k < counts[0]) & (tissue[k] > 0)

    def run(bricks, shifted, fine, pooled, head, patterns, pairs, sems, out_sems):
        def plane_copy(k, z):
            return pltpu.make_async_copy(embeddings.at[k, z], bricks.at[k, z], sems.at[k, z])

        def fine_copy(k):
            return pltpu.make_async_copy(fine.at[k], fine_ref.at[k], out_sems.at[k])

        for k in range(slots):

            @pl.when(running(k))
            def _():
                for z in range(depth):
                    plane_copy(k, z).start()

        for k in range(slots):

            @pl.when(jnp.logical_not(running(k)))
            def _():
                fine[k] = jnp.zeros((offsets, depth, height, width), bf16)
                fine_copy(k).start()

        write_patterns(patterns, pairs, channels)
        pooled[...] = jnp.zeros_like(pooled)
        lanes = iota((channels, width), 1)
        rows, columns = iota((POOL, width), 0), iota((POOL, width), 1)

        def do_slot(slot, carry):
            before = jnp.maximum(slot - 1, 0)
            left_ok = (slot > 0) & (tissue[before] > 0)
            free = {step: columns >= jnp.where(left_ok, 0, step) for step in SHIFTS}

            def prior_of(k):
                ahead = jnp.maximum(k - 1, 0)
                return jnp.where(running(ahead), ahead, k)

            def shift_row(k, z, y):
                own, prior = bricks[k, z, y], bricks[prior_of(k), z, y]
                for i, step in enumerate(SHIFTS):
                    joined = jnp.where(lanes >= width - step, prior, own)
                    shifted[i, z, y] = pltpu.roll(joined, step, 1)

            def plane(z, steps, final):
                if final:
                    after, next_z = jnp.minimum(slot + 1, slots - 1), 0

                    @pl.when((slot + 1 < slots) & running(after))
                    def _():
                        plane_copy(after, 0).wait()

                else:
                    after, next_z = slot, z + 1
                    plane_copy(slot, next_z).wait()
                pattern = pool_pattern(width)
                todo = list(range(height))
                units = 0
                for half in range(height // POOL):
                    first = half * POOL
                    centres = [bricks[slot, z, first + i] for i in range(POOL)]
                    (value,) = pooled_cells([centres], pattern)
                    place = (z * (height // POOL) + half) * channels
                    place = pl.ds(pl.multiple_of(place, channels), channels)
                    keep = lanes // cells == slot + 2
                    pooled[place, :] = jnp.where(keep, value.astype(bf16), pooled[place, :])
                    centre = lambda y: centres[y - first]

                    def partner_of(index):
                        step_z, _, step_x = FINE_OFFSETS[index]
                        if step_x:
                            k = SHIFTS.index(step_x)
                            return lambda y: shifted[k, z - step_z, y]
                        return lambda y: bricks[slot, z - step_z, y]

                    def finish(index, value):
                        _, step_y, step_x = FINE_OFFSETS[index]
                        inside = both(free.get(step_x), row_test(step_y, height, first, rows))
                        if inside is not None:
                            value = jnp.where(inside, value, 0.0)
                        fine[slot, index, z, first : first + POOL] = value.astype(bf16)

                    singles, doubles = [], []
                    for index, (step_z, step_y, _) in enumerate(FINE_OFFSETS):
                        start, stop = valid_rows(step_y, height, first)
                        if start >= stop or (step_z and step_z not in steps):
                            blank = jnp.zeros((POOL, width), bf16)
                            fine[slot, index, z, first : first + POOL] = blank
                        elif step_y in FOLDED:
                            doubles.append(index)
                        else:
                            singles.append(index)
                    if len(doubles) % 2:
                        singles.append(doubles.pop())
                    jobs = [(index,) for index in singles]
                    jobs += [tuple(doubles[i : i + 2]) for i in range(0, len(doubles), 2)]
                    jobs.sort(key=lambda job: FINE_OFFSETS[job[0]][2])
                    for job in jobs:
                        step_ys = [FINE_OFFSETS[index][1] for index in job]
                        partners = [partner_of(index) for index in job]
                        if len(job) == 1:
                            values = [
                                affinity_of(
                                    step_ys[0], height, first, patterns, centre, partners[0]
                                )
                            ]
                        else:
                            values = two_affinities(
                                step_ys, height, first, pairs, centre, partners
                            )
                        for index, value in zip(job, values):
                            finish(index, value)
                        units += len(job)
                        while todo and units >= 2 * (height - len(todo) + 1):
                            shift_row(after, next_z, todo.pop(0))
                for y in todo:
                    shift_row(after, next_z, y)

            @pl.when(running(slot) & ((slot == 0) | jnp.logical_not(running(before))))
            def _():
                plane_copy(slot, 0).wait()
                for y in range(height):
                    shift_row(slot, 0, y)

            @pl.when(running(slot))
            def _():
                last = depth - 1
                edges = sorted({0, last, depth} | {offset[0] for offset in FINE_OFFSETS})
                for low, high in zip(edges[:-1], edges[1:]):
                    steps = [offset[0] for offset in FINE_OFFSETS if 0 < offset[0] <= low]

                    def one(z, carry):
                        plane(z, steps, low == last)
                        return carry

                    lax.fori_loop(low, high, one, 0)
                fine_copy(slot).start()

            return carry

        lax.fori_loop(0, slots, do_slot, 0)

        @pl.when(running(0))
        def _():
            for group in range(depth // zs):
                for y in range(height):
                    values = [bricks[0, group * zs + j, y] for j in range(zs)]
                    place = (group * height + y) * channels
                    head[place : place + channels, :] = pack_rows(values, 0, lanes)

        pooled_copy = pltpu.make_async_copy(pooled, pooled_ref, out_sems.at[slots])
        head_copy = pltpu.make_async_copy(head, head_ref, out_sems.at[slots + 1])
        pooled_copy.start()
        head_copy.start()
        for k in range(slots):
            fine_copy(k).wait()
        pooled_copy.wait()
        head_copy.wait()

    pl.run_scoped(
        run,
        pltpu.VMEM((slots, depth, height, channels, width), bf16),
        pltpu.VMEM((len(SHIFTS), depth, height, channels, width), bf16),
        pltpu.VMEM((slots, offsets, depth, height, width), bf16),
        pltpu.VMEM((tiles * channels, width), bf16),
        pltpu.VMEM((depth // zs * height * channels, width), bf16),
        pltpu.VMEM((len(STARTS), POOL, POOL * channels // 2), bf16),
        pltpu.VMEM((len(STARTS) ** 2, 2 * POOL, POOL * channels // 2), bf16),
        pltpu.SemaphoreType.DMA((slots, depth)),
        pltpu.SemaphoreType.DMA((slots + 2,)),
    )


def join_kernel(
    counts, tissue, near_hbm, far_hbm, pooled_hbm, head_hbm, fine_in, fine_out, coarse_ref
):
    slots, cells_total = coarse_ref.shape
    _, offsets_fine, depth, height, width = fine_in.shape
    zs = width // PACK
    groups = depth // zs
    cells = width // POOL
    tiles = depth * height // POOL
    channels = head_hbm.shape[0] // (groups * height)
    per_row = width // (2 * cells)
    rim_rows = groups * height * channels
    pool_rows = tiles // per_row * channels

    def run(near_ref, far_ref, pooled_ref, head_ref, fine, turned, patterns, pairs, sems):
        active = tissue[0] > 0
        fetches = [
            pltpu.make_async_copy(source, target, sems.at[k])
            for k, (source, target) in enumerate(
                (
                    (near_hbm, near_ref),
                    (far_hbm, far_ref),
                    (pooled_hbm, pooled_ref),
                    (head_hbm, head_ref),
                    (fine_in.at[0], fine),
                )
            )
        ]
        store = pltpu.make_async_copy(fine, fine_out.at[0], sems.at[5])
        for fetch in fetches:
            fetch.start()
        lanes = iota((channels, width), 1)
        write_patterns(patterns, pairs, channels)
        fetches[0].wait()
        fetches[1].wait()
        near_flags = near_ref[rim_rows + pool_rows :, :].astype(jnp.float32)
        far_flags = far_ref[pool_rows:, :].astype(jnp.float32)
        near_mark, second_mark, has_two = near_flags[0:1], near_flags[1:2], near_flags[2:3]
        far_mark = jnp.where(has_two > 0, second_mark, far_flags[0:1])

        @pl.when(active)
        def _():
            def rim(group, y):
                row = (group * height + y) * channels
                return near_ref[row : row + channels, :]

            def head(group, y):
                row = (group * height + y) * channels
                return head_ref[row : row + channels, :]

            for k, (step_x, step_z) in enumerate(RIM_TURNS):
                shift = (step_x + PACK * step_z - PACK) % width
                for y in range(height):
                    held = None
                    for group in range(groups):
                        value = pltpu.roll(rim(group, y), shift, 1)
                        fresh = value
                        if held is not None and step_z:
                            fresh = jnp.where(lanes < PACK * step_z, held, value)
                        turned[k, group, y] = fresh
                        held = value
            fetches[3].wait()
            fetches[4].wait()
            rows, columns = iota((POOL, width), 0), iota((POOL, width), 1)
            near_rows = jnp.broadcast_to(near_mark, (POOL, width)) > 0
            for group in range(groups):
                for first in range(0, height, POOL):
                    centres = [head(group, first + i) for i in range(POOL)]
                    for index, (step_z, step_y, step_x) in enumerate(FINE_OFFSETS):
                        start, stop = valid_rows(step_y, height, first)
                        if step_x == 0 or (group + 1) * zs <= step_z or start >= stop:
                            continue
                        if step_z >= zs:
                            turn, source = RIM_TURNS.index((step_x, 0)), group - step_z // zs
                        else:
                            turn, source = RIM_TURNS.index((step_x, step_z)), group
                        value = affinity_of(
                            step_y,
                            height,
                            first,
                            patterns,
                            lambda y: centres[y - first],
                            lambda y: turned[turn, source, y],
                        )
                        inside = both(near_rows, row_test(step_y, height, first, rows))
                        value = jnp.where(inside, value, 0.0)
                        for j in range(zs):
                            z = group * zs + j
                            if z < step_z:
                                continue
                            moved = value
                            if j:
                                moved = pltpu.roll(value, width - PACK * j, 1)
                            place = fine.at[index, z, first : first + POOL]
                            old = place[...].astype(jnp.float32)
                            fresh = jnp.where(columns < step_x, moved, old)
                            place[...] = fresh.astype(jnp.bfloat16)
            store.start()

        fetches[2].wait()
        out_x = iota((1, width), 1)
        mark = jnp.where(out_x < cells, far_mark, near_mark)
        for k in range(slots):
            own = jnp.where((k < counts[0]) & (tissue[k] > 0), 1.0, 0.0)
            mark = jnp.where(out_x >= (k + 2) * cells, own, mark)
        mark = jnp.where(out_x >= (slots + 2) * cells, 0.0, mark)
        offsets = (CO_NEAR, CO_FAR)
        scores = [[] for _ in offsets]
        for tile in range(tiles):
            block, part = tile // per_row, tile % per_row
            near_rows = slice(rim_rows + block * channels, rim_rows + (block + 1) * channels)
            far_rows = slice(block * channels, (block + 1) * channels)
            near = near_ref[near_rows, :]
            if part:
                near = pltpu.roll(near, width - 2 * part * cells, 1)
            far = pltpu.roll(far_ref[far_rows, :], width - (2 * part + 1) * cells, 1)
            far = jnp.where((has_two <= 0) & (lanes < cells), far.astype(jnp.float32), near.astype(jnp.float32))
            own = pooled_ref[tile * channels : (tile + 1) * channels, :].astype(jnp.float32)
            row = jnp.where(lanes < 2 * cells, far, own)
            for k, offset in enumerate(offsets):
                scores[k].append(jnp.sum(row * pltpu.roll(row, offset, 1), axis=0, keepdims=True))
        tables = []
        for k, offset in enumerate(offsets):
            score = jnp.concatenate(scores[k], 0)
            weight = mark * pltpu.roll(mark, offset, 1)
            value = 0.5 * jnp.tanh(score * (0.5 / math.sqrt(channels))) + 0.5
            tables.append(value * weight)
        table = jnp.concatenate(tables, 0).astype(jnp.bfloat16)
        count = table.shape[0]
        source, target = iota((width, cells_total), 0), iota((width, cells_total), 1)
        chosen = iota((count, cells_total), 0) == iota((count, cells_total), 1) // cells
        for k in range(slots):
            pick = jnp.where(source == (k + 2) * cells + target % cells, 1.0, 0.0)
            spread = jnp.dot(table, pick.astype(jnp.bfloat16), preferred_element_type=jnp.float32)
            line = jnp.sum(jnp.where(chosen, spread, 0.0), axis=0, keepdims=True)
            coarse_ref[k : k + 1, :] = line.astype(jnp.bfloat16)

        @pl.when(active)
        def _():
            store.wait()

        @pl.when(jnp.logical_not(active))
        def _():
            fetches[3].wait()
            fetches[4].wait()

    half = jnp.bfloat16
    pl.run_scoped(
        run,
        pltpu.VMEM(near_hbm.shape, half),
        pltpu.VMEM(far_hbm.shape, half),
        pltpu.VMEM(pooled_hbm.shape, half),
        pltpu.VMEM(head_hbm.shape, half),
        pltpu.VMEM((offsets_fine, depth, height, width), half),
        pltpu.VMEM((len(RIM_TURNS), groups, height, channels, width), half),
        pltpu.VMEM((len(STARTS), POOL, POOL * channels // 2), half),
        pltpu.VMEM((len(STARTS) ** 2, 2 * POOL, POOL * channels // 2), half),
        pltpu.SemaphoreType.DMA((6,)),
    )


def body(embeddings, tissue, counts):
    slots, depth, height, channels, width = embeddings.shape
    offsets = len(FINE_OFFSETS)
    cells = width // POOL
    tiles = depth * height // POOL
    groups = depth // (width // PACK)
    rim_rows = groups * height * channels
    pool_rows = tiles * 2 * cells // width * channels
    smem = pl.BlockSpec(memory_space=pltpu.SMEM)
    anyspace = pl.BlockSpec(memory_space=pl.ANY)
    vmem = pl.BlockSpec(memory_space=pltpu.VMEM)
    half = jnp.bfloat16
    big = 60 * 1024 * 1024

    send, far = pl.pallas_call(
        send_kernel,
        out_shape=(
            jax.ShapeDtypeStruct((rim_rows + pool_rows + 16, width), half),
            jax.ShapeDtypeStruct((pool_rows + 16, width), half),
        ),
        in_specs=[smem, smem, anyspace],
        out_specs=(anyspace, anyspace),
        compiler_params=pltpu.CompilerParams(vmem_limit_bytes=big),
        name="send",
    )(counts, tissue, embeddings)

    axes = ("gz", "ba")
    devices = lax.axis_size(axes)
    near_in = lax.ppermute(send, axes, [(d, d + 1) for d in range(devices - 1)])
    far_in = lax.ppermute(far, axes, [(d, d + 2) for d in range(devices - 2)])

    fine, pooled, head = pl.pallas_call(
        fine_kernel,
        out_shape=(
            jax.ShapeDtypeStruct((slots, offsets, depth, height, width), half),
            jax.ShapeDtypeStruct((tiles * channels, width), half),
            jax.ShapeDtypeStruct((rim_rows, width), half),
        ),
        in_specs=[smem, smem, anyspace],
        out_specs=(anyspace, anyspace, anyspace),
        compiler_params=pltpu.CompilerParams(vmem_limit_bytes=big),
        cost_estimate=pl.CostEstimate(
            flops=20_000_000_000, bytes_accessed=20_000_000, transcendentals=0
        ),
        name="fine",
    )(counts, tissue, embeddings)

    return pl.pallas_call(
        join_kernel,
        out_shape=(
            jax.ShapeDtypeStruct(fine.shape, half),
            jax.ShapeDtypeStruct((slots, 2 * tiles * cells), half),
        ),
        in_specs=[smem, smem] + [anyspace] * 5,
        out_specs=(anyspace, vmem),
        input_output_aliases={6: 0},
        compiler_params=pltpu.CompilerParams(vmem_limit_bytes=big),
        name="join",
    )(counts, tissue, near_in, far_in, pooled, head, fine)


def solution(mesh):
    in_specs = (P(("gz", "ba"), None, None, None, None), P(("gz", "ba")), P(("gz", "ba")))
    out_specs = (P(("gz", "ba"), None, None, None, None), P(("gz", "ba"), None))
    return jax.shard_map(body, mesh=mesh, in_specs=in_specs, out_specs=out_specs, check_vma=False)
```

```python
import math

import jax
import jax.numpy as jnp
from jax import lax
from jax.experimental import pallas as pl
from jax.experimental.pallas import tpu as pltpu
from jax.sharding import PartitionSpec as P

CO_NEAR = 10
CO_FAR = 30
POOL = 8
PACK = 32

FINE_OFFSETS = (
    (0, 0, 1),
    (0, 0, 3),
    (0, 0, 9),
    (0, 0, 27),
    (0, 1, 0),
    (0, 3, 0),
    (0, 9, 0),
    (1, 0, 0),
    (2, 0, 0),
    (4, 0, 0),
    (0, 1, 1),
    (0, 3, 3),
    (0, 9, 9),
    (0, 9, 27),
    (0, -1, 1),
    (0, -3, 3),
    (0, -9, 9),
    (0, -9, 27),
    (1, 0, 3),
    (2, 0, 9),
    (4, 0, 27),
    (1, 1, 0),
    (2, 3, 0),
    (4, 9, 0),
    (1, 1, 1),
    (2, 3, 9),
)
SHIFTS = (1, 3, 9, 27)
STARTS = (0, 1, 3)
PLANES = 4
FOLDED = (0, 1, -1, 3, -3, 9, -9)
RIM_TURNS = ((1, 0), (3, 0), (9, 0), (27, 0), (3, 1), (1, 1), (9, 2))


def iota(shape, dim):
    return lax.broadcasted_iota(jnp.int32, shape, dim)


def write_patterns(ref, pair_ref, channels):
    _, rows, width = ref.shape
    scale = 0.5 / math.sqrt(channels)
    for k, start in enumerate(STARTS):
        hit = iota((rows, width), 1) // (channels // 2) + start == iota((rows, width), 0)
        ref[k] = jnp.where(hit, scale, 0.0).astype(jnp.bfloat16)
    row, column = iota((2 * rows, width), 0), iota((2 * rows, width), 1)
    place = column // (channels // 4)
    for i, low in enumerate(STARTS):
        for j, high in enumerate(STARTS):
            start = jnp.where(place < rows, low, high)
            hit = (place % rows + start == row % rows) & (place // rows == row // rows)
            pair_ref[i * len(STARTS) + j] = jnp.where(hit, scale, 0.0).astype(jnp.bfloat16)


def folded_product(left, right, levels):
    product = left * right
    for _ in range(levels):
        half = product.shape[0] // 2
        product = product[:half] + product[half:]
    return product


def valid_rows(step_y, height, first):
    start = max(first, step_y, 0)
    stop = min(first + POOL, height + min(step_y, 0))
    return start, stop


def stacked_products(step_y, height, first, levels, centre, partner):
    start, stop = valid_rows(step_y, height, first)
    products = [folded_product(centre(y), partner(y - step_y), levels) for y in range(start, stop)]
    blank = jnp.zeros_like(products[0])
    return products + [blank] * (POOL - len(products)), STARTS.index(start - first)


def mask_keys(height):
    keys = []
    for _, step_y, step_x in FINE_OFFSETS:
        for first in range(0, height, POOL):
            start, stop = valid_rows(step_y, height, first)
            key = (step_x, start - first, stop - first)
            if start < stop and key not in keys:
                keys.append(key)
    return keys


def affinity_of(step_y, height, first, patterns, centre, partner):
    products, start = stacked_products(step_y, height, first, 1, centre, partner)
    products = jnp.concatenate(products, 0)
    return jnp.tanh(jnp.dot(patterns[start], products, preferred_element_type=jnp.float32))


def two_affinities(step_ys, height, first, patterns, centre, partners):
    products, starts = [], []
    for step_y, partner in zip(step_ys, partners):
        more, start = stacked_products(step_y, height, first, 2, centre, partner)
        products += more
        starts.append(start)
    pattern = patterns[starts[0] * len(STARTS) + starts[1]]
    products = jnp.concatenate(products, 0)
    value = jnp.tanh(jnp.dot(pattern, products, preferred_element_type=jnp.float32))
    return value[:POOL], value[POOL:]


def row_test(step_y, height, first, rows):
    start, stop = valid_rows(step_y, height, first)
    test = None
    if start > first:
        test = rows >= start - first
    if stop < first + POOL:
        upper = rows < stop - first
        test = upper if test is None else test & upper
    return test


def both(left, right):
    if left is None or right is None:
        return left if right is None else right
    return left & right


def pool_pattern(width):
    k, lane = iota((width, width), 0), iota((width, width), 1)
    hit = k // POOL == lane % (width // POOL)
    return jnp.where(hit, 1.0 / (POOL * POOL), 0.0).astype(jnp.bfloat16)


def pooled_cells(blocks, pattern):
    channels = blocks[0][0].shape[0]
    pairs = [
        jnp.concatenate([rows[i], rows[i + 1]], 1)
        for rows in blocks
        for i in range(0, POOL, 2)
    ]
    spread = jnp.concatenate([pattern, pattern], 0)
    parts = jnp.dot(jnp.concatenate(pairs, 0), spread, preferred_element_type=jnp.float32)
    results = []
    for k in range(len(blocks)):
        average = None
        for i in range(POOL // 2):
            place = (k * (POOL // 2) + i) * channels
            part = parts[place : place + channels]
            average = part if average is None else average + part
        mean = jnp.mean(average * average, axis=0, keepdims=True)
        results.append(average * lax.rsqrt(mean + 1e-6))
    return results


def pack_rows(values, turn, lanes):
    group = lanes // PACK
    width = lanes.shape[1]
    result = None
    for j, value in enumerate(values):
        shift = (PACK * j + turn) % width
        if shift:
            value = pltpu.roll(value, shift, 1)
        result = value if result is None else jnp.where(group == j, value, result)
    return result


def send_kernel(counts, tissue, embeddings, send_ref, far_ref):
    _, depth, height, channels, width = embeddings.shape
    cells = width // POOL
    tiles = depth * height // POOL
    per_row = width // (2 * cells)
    zs = width // PACK
    rim_rows = depth // zs * height * channels
    pool_rows = tiles // per_row * channels

    def run(bricks, sems):
        count = counts[0]
        last = count - 1
        second = jnp.maximum(count - 2, 0)
        copies = {}
        for z in range(depth):
            for k, slot in enumerate((last, second)):
                copy = pltpu.make_async_copy(embeddings.at[slot, z], bricks.at[k, z], sems.at[k, z])
                copy.start()
                copies[k, z] = copy
        lanes = iota((channels, width), 1)
        pattern = pool_pattern(width)
        own_mark = tissue[last].astype(jnp.float32)
        has_two = (count >= 2).astype(jnp.float32)
        second_mark = tissue[second].astype(jnp.float32) * has_two
        row = iota((16, width), 0)
        flags = jnp.where(row == 0, own_mark, jnp.where(row == 1, second_mark, has_two))
        send_ref[rim_rows + pool_rows :, :] = flags.astype(jnp.bfloat16)
        far_ref[pool_rows:, :] = flags.astype(jnp.bfloat16)
        planes = per_row * POOL // height
        for group in range(depth // zs):
            for z in range(group * zs, group * zs + zs):
                copies[0, z].wait()
                copies[1, z].wait()
            for y in range(height):
                values = [bricks[0, group * zs + j, y] for j in range(zs)]
                place = (group * height + y) * channels
                send_ref[place : place + channels, :] = pack_rows(values, PACK, lanes)
            for block in range(group * zs // planes, (group + 1) * zs // planes):
                total = jnp.zeros((channels, width), jnp.float32)
                for part in range(per_row):
                    tile = block * per_row + part
                    z, y0 = tile // (height // POOL), tile % (height // POOL) * POOL
                    blocks = [[bricks[k, z, y0 + i] for i in range(POOL)] for k in range(2)]
                    for k, value in enumerate(pooled_cells(blocks, pattern)):
                        total = jnp.where(lanes // cells == 2 * part + 1 - k, value, total)
                total = total.astype(jnp.bfloat16)
                place = block * channels
                far_ref[place : place + channels, :] = total
                send_ref[rim_rows + place : rim_rows + place + channels, :] = total

    pl.run_scoped(
        run,
        pltpu.VMEM((2, depth, height, channels, width), jnp.bfloat16),
        pltpu.SemaphoreType.DMA((2, depth)),
    )


def fine_kernel(counts, tissue, embeddings, fine_ref, pooled, head):
    slots, depth, height, channels, width = embeddings.shape
    offsets = len(FINE_OFFSETS)
    cells = width // POOL
    tiles = depth * height // POOL
    zs = width // PACK
    bf16 = jnp.bfloat16

    def running(k):
        return (k < counts[0]) & (tissue[k] > 0)

    def run(bricks, shifted, fine, patterns, pairs, weights, sems, out_sems):
        def plane_copy(k, z):
            return pltpu.make_async_copy(embeddings.at[k, z], bricks.at[k, z], sems.at[k, z])

        def fine_copy(k):
            return pltpu.make_async_copy(fine.at[k], fine_ref.at[k], out_sems.at[k])

        for k in range(slots):

            @pl.when(running(k))
            def _():
                for z in range(depth):
                    plane_copy(k, z).start()

        for k in range(slots):

            @pl.when(jnp.logical_not(running(k)))
            def _():
                fine[k] = jnp.zeros((offsets, depth, height, width), bf16)
                fine_copy(k).start()

        write_patterns(patterns, pairs, channels)
        pooled[...] = jnp.zeros_like(pooled)
        lanes = iota((channels, width), 1)
        rows, columns = iota((POOL, width), 0), iota((POOL, width), 1)
        keys = mask_keys(height)

        def do_slot(slot, carry):
            before = jnp.maximum(slot - 1, 0)
            left_ok = (slot > 0) & (tissue[before] > 0)
            for k, (step_x, start, stop) in enumerate(keys):
                inside = columns >= jnp.where(left_ok, 0, step_x)
                inside = inside & (rows >= start) & (rows < stop)
                weights[k] = jnp.where(inside, 0.5, 0.0)

            def prior_of(k):
                ahead = jnp.maximum(k - 1, 0)
                return jnp.where(running(ahead), ahead, k)

            def shift_row(k, z, y):
                own, prior = bricks[k, z, y], bricks[prior_of(k), z, y]
                for i, step in enumerate(SHIFTS):
                    joined = jnp.where(lanes >= width - step, prior, own)
                    shifted[i, z, y] = pltpu.roll(joined, step, 1)

            def plane(z, steps, final):
                if final:
                    after, next_z = jnp.minimum(slot + 1, slots - 1), 0
                else:
                    after, next_z = slot, z + 1
                pattern = pool_pattern(width)
                todo = list(range(height))
                units = 0
                for half in range(height // POOL):
                    first = half * POOL
                    centres = [bricks[slot, z, first + i] for i in range(POOL)]
                    (value,) = pooled_cells([centres], pattern)
                    place = (z * (height // POOL) + half) * channels
                    place = pl.ds(place, channels)
                    keep = lanes // cells == slot + 2
                    pooled[place, :] = jnp.where(keep, value.astype(bf16), pooled[place, :])
                    centre = lambda y: centres[y - first]

                    def partner_of(index):
                        step_z, _, step_x = FINE_OFFSETS[index]
                        if step_x:
                            k = SHIFTS.index(step_x)
                            return lambda y: shifted[k, z - step_z, y]
                        return lambda y: bricks[slot, z - step_z, y]

                    def finish(index, value):
                        _, step_y, step_x = FINE_OFFSETS[index]
                        start, stop = valid_rows(step_y, height, first)
                        weight = weights[keys.index((step_x, start - first, stop - first))]
                        value = value * weight + weight
                        fine[slot, index, z, first : first + POOL] = value.astype(bf16)

                    singles, doubles = [], []
                    for index, (step_z, step_y, _) in enumerate(FINE_OFFSETS):
                        start, stop = valid_rows(step_y, height, first)
                        if start >= stop or (step_z and step_z not in steps):
                            blank = jnp.zeros((POOL, width), bf16)
                            fine[slot, index, z, first : first + POOL] = blank
                        elif step_y in FOLDED:
                            doubles.append(index)
                        else:
                            singles.append(index)
                    if len(doubles) % 2:
                        singles.append(doubles.pop())
                    jobs = [(index,) for index in singles]
                    jobs += [tuple(doubles[i : i + 2]) for i in range(0, len(doubles), 2)]
                    jobs.sort(key=lambda job: FINE_OFFSETS[job[0]][2])
                    for job in jobs:
                        step_ys = [FINE_OFFSETS[index][1] for index in job]
                        partners = [partner_of(index) for index in job]
                        if len(job) == 1:
                            values = [
                                affinity_of(
                                    step_ys[0], height, first, patterns, centre, partners[0]
                                )
                            ]
                        else:
                            values = two_affinities(
                                step_ys, height, first, pairs, centre, partners
                            )
                        for index, value in zip(job, values):
                            finish(index, value)
                        units += len(job)
                        while todo and units >= 2 * (height - len(todo) + 1):
                            shift_row(after, next_z, todo.pop(0))
                for y in todo:
                    shift_row(after, next_z, y)

            @pl.when(running(slot) & ((slot == 0) | jnp.logical_not(running(before))))
            def _():
                plane_copy(slot, 0).wait()
                for y in range(height):
                    shift_row(slot, 0, y)

            @pl.when(running(slot))
            def _():
                last = depth - 1
                follower = jnp.minimum(slot + 1, slots - 1)
                for low in range(0, depth, PLANES):
                    for z in range(low + 1, min(low + PLANES, last) + 1):
                        plane_copy(slot, z).wait()
                    if low + PLANES >= depth:

                        @pl.when((slot + 1 < slots) & running(follower))
                        def _():
                            plane_copy(follower, 0).wait()

                    for z in range(low, low + PLANES):
                        steps = [offset[0] for offset in FINE_OFFSETS if 0 < offset[0] <= z]
                        plane(z, steps, z == last)

                fine_copy(slot).start()

            return carry

        lax.fori_loop(0, slots, do_slot, 0)

        @pl.when(running(0))
        def _():
            for group in range(depth // zs):
                for y in range(height):
                    values = [bricks[0, group * zs + j, y] for j in range(zs)]
                    place = (group * height + y) * channels
                    head[place : place + channels, :] = pack_rows(values, 0, lanes)

        for k in range(slots):
            fine_copy(k).wait()

    pl.run_scoped(
        run,
        pltpu.VMEM((slots, depth, height, channels, width), bf16),
        pltpu.VMEM((len(SHIFTS), depth, height, channels, width), bf16),
        pltpu.VMEM((slots, offsets, depth, height, width), bf16),
        pltpu.VMEM((len(STARTS), POOL, POOL * channels // 2), bf16),
        pltpu.VMEM((len(STARTS) ** 2, 2 * POOL, POOL * channels // 2), bf16),
        pltpu.VMEM((len(mask_keys(height)), POOL, width), jnp.float32),
        pltpu.SemaphoreType.DMA((slots, depth)),
        pltpu.SemaphoreType.DMA((slots,)),
    )


def join_kernel(
    counts, tissue, near_ref, far_ref, pooled_ref, head_ref, fine_in, fine_out, coarse_ref
):
    slots, cells_total = coarse_ref.shape
    _, offsets_fine, depth, height, width = fine_in.shape
    zs = width // PACK
    groups = depth // zs
    cells = width // POOL
    tiles = depth * height // POOL
    channels = head_ref.shape[0] // (groups * height)
    per_row = width // (2 * cells)
    rim_rows = groups * height * channels
    pool_rows = tiles // per_row * channels

    def run(fine, turned, patterns, pairs, sems):
        active = tissue[0] > 0
        fetch = pltpu.make_async_copy(fine_in.at[0], fine, sems.at[0])
        store = pltpu.make_async_copy(fine, fine_out.at[0], sems.at[1])

        @pl.when(active)
        def _():
            fetch.start()

        lanes = iota((channels, width), 1)
        write_patterns(patterns, pairs, channels)
        near_flags = near_ref[rim_rows + pool_rows :, :].astype(jnp.float32)
        far_flags = far_ref[pool_rows:, :].astype(jnp.float32)
        near_mark, second_mark, has_two = near_flags[0:1], near_flags[1:2], near_flags[2:3]
        far_mark = jnp.where(has_two > 0, second_mark, far_flags[0:1])

        @pl.when(active)
        def _():
            def rim(group, y):
                row = (group * height + y) * channels
                return near_ref[row : row + channels, :]

            def head(group, y):
                row = (group * height + y) * channels
                return head_ref[row : row + channels, :]

            for y in range(height):
                rims = [rim(group, y) for group in range(groups)]
                for k, (step_x, step_z) in enumerate(RIM_TURNS):
                    shift = (step_x + PACK * step_z - PACK) % width
                    held = None
                    for group in range(groups):
                        value = pltpu.roll(rims[group], shift, 1)
                        fresh = value
                        if held is not None and step_z:
                            fresh = jnp.where(lanes < PACK * step_z, held, value)
                        turned[k, group, y] = fresh
                        held = value
            fetch.wait()
            rows, columns = iota((POOL, width), 0), iota((POOL, width), 1)
            near_rows = jnp.broadcast_to(near_mark, (POOL, width)) > 0
            for group in range(groups):
                for first in range(0, height, POOL):
                    centres = [head(group, first + i) for i in range(POOL)]
                    for index, (step_z, step_y, step_x) in enumerate(FINE_OFFSETS):
                        start, stop = valid_rows(step_y, height, first)
                        if step_x == 0 or (group + 1) * zs <= step_z or start >= stop:
                            continue
                        if step_z >= zs:
                            turn, source = RIM_TURNS.index((step_x, 0)), group - step_z // zs
                        else:
                            turn, source = RIM_TURNS.index((step_x, step_z)), group
                        value = affinity_of(
                            step_y,
                            height,
                            first,
                            patterns,
                            lambda y: centres[y - first],
                            lambda y: turned[turn, source, y],
                        )
                        inside = both(near_rows, row_test(step_y, height, first, rows))
                        value = jnp.where(inside, 0.5 * value + 0.5, 0.0)
                        for j in range(zs):
                            z = group * zs + j
                            if z < step_z:
                                continue
                            moved = value
                            if j:
                                moved = pltpu.roll(value, width - PACK * j, 1)
                            place = fine.at[index, z, first : first + POOL]
                            old = place[...].astype(jnp.float32)
                            fresh = jnp.where(columns < step_x, moved, old)
                            place[...] = fresh.astype(jnp.bfloat16)
            store.start()

        out_x = iota((1, width), 1)
        mark = jnp.where(out_x < cells, far_mark, near_mark)
        for k in range(slots):
            own = jnp.where((k < counts[0]) & (tissue[k] > 0), 1.0, 0.0)
            mark = jnp.where(out_x >= (k + 2) * cells, own, mark)
        mark = jnp.where(out_x >= (slots + 2) * cells, 0.0, mark)
        offsets = (CO_NEAR, CO_FAR)
        scores = [[] for _ in offsets]
        for tile in range(tiles):
            block, part = tile // per_row, tile % per_row
            near_rows = slice(rim_rows + block * channels, rim_rows + (block + 1) * channels)
            far_rows = slice(block * channels, (block + 1) * channels)
            near = near_ref[near_rows, :]
            if part:
                near = pltpu.roll(near, width - 2 * part * cells, 1)
            far = pltpu.roll(far_ref[far_rows, :], width - (2 * part + 1) * cells, 1)
            far = jnp.where((has_two <= 0) & (lanes < cells), far.astype(jnp.float32), near.astype(jnp.float32))
            own = pooled_ref[tile * channels : (tile + 1) * channels, :].astype(jnp.float32)
            row = jnp.where(lanes < 2 * cells, far, own)
            for k, offset in enumerate(offsets):
                scores[k].append(jnp.sum(row * pltpu.roll(row, offset, 1), axis=0, keepdims=True))
        tables = []
        for k, offset in enumerate(offsets):
            score = jnp.concatenate(scores[k], 0)
            weight = mark * pltpu.roll(mark, offset, 1)
            value = 0.5 * jnp.tanh(score * (0.5 / math.sqrt(channels))) + 0.5
            tables.append(value * weight)
        table = jnp.concatenate(tables, 0).astype(jnp.bfloat16)
        count = table.shape[0]
        source, target = iota((width, cells_total), 0), iota((width, cells_total), 1)
        chosen = iota((count, cells_total), 0) == iota((count, cells_total), 1) // cells
        for k in range(slots):
            pick = jnp.where(source == (k + 2) * cells + target % cells, 1.0, 0.0)
            spread = jnp.dot(table, pick.astype(jnp.bfloat16), preferred_element_type=jnp.float32)
            line = jnp.sum(jnp.where(chosen, spread, 0.0), axis=0, keepdims=True)
            coarse_ref[k : k + 1, :] = line.astype(jnp.bfloat16)

        @pl.when(active)
        def _():
            store.wait()

    half = jnp.bfloat16
    pl.run_scoped(
        run,
        pltpu.VMEM((offsets_fine, depth, height, width), half),
        pltpu.VMEM((len(RIM_TURNS), groups, height, channels, width), half),
        pltpu.VMEM((len(STARTS), POOL, POOL * channels // 2), half),
        pltpu.VMEM((len(STARTS) ** 2, 2 * POOL, POOL * channels // 2), half),
        pltpu.SemaphoreType.DMA((2,)),
    )


def body(embeddings, tissue, counts):
    slots, depth, height, channels, width = embeddings.shape
    offsets = len(FINE_OFFSETS)
    cells = width // POOL
    tiles = depth * height // POOL
    groups = depth // (width // PACK)
    rim_rows = groups * height * channels
    pool_rows = tiles * 2 * cells // width * channels
    smem = pl.BlockSpec(memory_space=pltpu.SMEM)
    anyspace = pl.BlockSpec(memory_space=pl.ANY)
    vmem = pl.BlockSpec(memory_space=pltpu.VMEM)
    half = jnp.bfloat16
    big = 40 * 1024 * 1024

    embeddings = pltpu.with_memory_space_constraint(embeddings, pltpu.HBM)
    send, far = pl.pallas_call(
        send_kernel,
        out_shape=(
            pltpu.VMEM((rim_rows + pool_rows + 16, width), half),
            pltpu.VMEM((pool_rows + 16, width), half),
        ),
        in_specs=[smem, smem, anyspace],
        out_specs=(vmem, vmem),
        compiler_params=pltpu.CompilerParams(vmem_limit_bytes=big),
        name="send",
    )(counts, tissue, embeddings)

    axes = ("gz", "ba")
    devices = lax.axis_size(axes)
    near_in = lax.ppermute(send, axes, [(d, d + 1) for d in range(devices - 1)])
    far_in = lax.ppermute(far, axes, [(d, d + 2) for d in range(devices - 2)])

    fine, pooled, head = pl.pallas_call(
        fine_kernel,
        out_shape=(
            jax.ShapeDtypeStruct((slots, offsets, depth, height, width), half),
            pltpu.VMEM((tiles * channels, width), half),
            pltpu.VMEM((rim_rows, width), half),
        ),
        in_specs=[smem, smem, anyspace],
        out_specs=(anyspace, vmem, vmem),
        compiler_params=pltpu.CompilerParams(vmem_limit_bytes=big),
        cost_estimate=pl.CostEstimate(
            flops=20_000_000_000, bytes_accessed=20_000_000, transcendentals=0
        ),
        name="fine",
    )(counts, tissue, embeddings)

    near_in, far_in, pooled, head = (
        pltpu.with_memory_space_constraint(value, pltpu.VMEM)
        for value in (near_in, far_in, pooled, head)
    )
    return pl.pallas_call(
        join_kernel,
        out_shape=(
            jax.ShapeDtypeStruct(fine.shape, half),
            jax.ShapeDtypeStruct((slots, 2 * tiles * cells), half),
        ),
        in_specs=[smem, smem] + [vmem] * 4 + [anyspace],
        out_specs=(anyspace, vmem),
        input_output_aliases={6: 0},
        compiler_params=pltpu.CompilerParams(vmem_limit_bytes=big),
        name="join",
    )(counts, tissue, near_in, far_in, pooled, head, fine)


def solution(mesh):
    in_specs = (P(("gz", "ba"), None, None, None, None), P(("gz", "ba")), P(("gz", "ba")))
    out_specs = (P(("gz", "ba"), None, None, None, None), P(("gz", "ba"), None))
    return jax.shard_map(body, mesh=mesh, in_specs=in_specs, out_specs=out_specs, check_vma=False)
```

```python
import math

import jax
import jax.numpy as jnp
from jax import lax
from jax.experimental import pallas as pl
from jax.experimental.pallas import tpu as pltpu
from jax.sharding import PartitionSpec as P

CO_NEAR = 10
CO_FAR = 30
POOL = 8
PACK = 32

FINE_OFFSETS = (
    (0, 0, 1),
    (0, 0, 3),
    (0, 0, 9),
    (0, 0, 27),
    (0, 1, 0),
    (0, 3, 0),
    (0, 9, 0),
    (1, 0, 0),
    (2, 0, 0),
    (4, 0, 0),
    (0, 1, 1),
    (0, 3, 3),
    (0, 9, 9),
    (0, 9, 27),
    (0, -1, 1),
    (0, -3, 3),
    (0, -9, 9),
    (0, -9, 27),
    (1, 0, 3),
    (2, 0, 9),
    (4, 0, 27),
    (1, 1, 0),
    (2, 3, 0),
    (4, 9, 0),
    (1, 1, 1),
    (2, 3, 9),
)
SHIFTS = (1, 3, 9, 27)
STARTS = (0, 1, 3)
PLANES = 4
FOLDED = (0, 1, -1, 3, -3, 9, -9)
RIM_TURNS = ((1, 0), (3, 0), (9, 0), (27, 0), (3, 1), (1, 1), (9, 2))


def iota(shape, dim):
    return lax.broadcasted_iota(jnp.int32, shape, dim)


def write_patterns(ref, pair_ref, channels):
    _, rows, width = ref.shape
    scale = 0.5 / math.sqrt(channels)
    for k, start in enumerate(STARTS):
        hit = iota((rows, width), 1) // (channels // 2) + start == iota((rows, width), 0)
        ref[k] = jnp.where(hit, scale, 0.0).astype(jnp.bfloat16)
    row, column = iota((2 * rows, width), 0), iota((2 * rows, width), 1)
    place = column // (channels // 4)
    for i, low in enumerate(STARTS):
        for j, high in enumerate(STARTS):
            start = jnp.where(place < rows, low, high)
            hit = (place % rows + start == row % rows) & (place // rows == row // rows)
            pair_ref[i * len(STARTS) + j] = jnp.where(hit, scale, 0.0).astype(jnp.bfloat16)


def folded_product(left, right, levels):
    product = left * right
    for _ in range(levels):
        half = product.shape[0] // 2
        product = product[:half] + product[half:]
    return product


def valid_rows(step_y, height, first):
    start = max(first, step_y, 0)
    stop = min(first + POOL, height + min(step_y, 0))
    return start, stop


def stacked_products(step_y, height, first, levels, centre, partner):
    start, stop = valid_rows(step_y, height, first)
    products = [folded_product(centre(y), partner(y - step_y), levels) for y in range(start, stop)]
    blank = jnp.zeros_like(products[0])
    return products + [blank] * (POOL - len(products)), STARTS.index(start - first)


def mask_keys(height):
    keys = []
    for _, step_y, step_x in FINE_OFFSETS:
        for first in range(0, height, POOL):
            start, stop = valid_rows(step_y, height, first)
            key = (step_x, start - first, stop - first)
            if start < stop and key not in keys:
                keys.append(key)
    return keys


def affinity_of(step_y, height, first, patterns, centre, partner):
    products, start = stacked_products(step_y, height, first, 1, centre, partner)
    products = jnp.concatenate(products, 0)
    return jnp.tanh(jnp.dot(patterns[start], products, preferred_element_type=jnp.float32))


def write_sums(ref, channels):
    rows, width = ref.shape
    hit = iota((rows, width), 1) // (width // rows) == iota((rows, width), 0)
    ref[...] = jnp.where(hit, 0.5 / math.sqrt(channels), 0.0).astype(jnp.bfloat16)


def two_affinities(step_ys, height, first, patterns, centre, partners):
    products, starts = [], []
    for step_y, partner in zip(step_ys, partners):
        more, start = stacked_products(step_y, height, first, 2, centre, partner)
        products += more
        starts.append(start)
    pattern = patterns[starts[0] * len(STARTS) + starts[1]]
    products = jnp.concatenate(products, 0)
    value = jnp.tanh(jnp.dot(pattern, products, preferred_element_type=jnp.float32))
    return value[:POOL], value[POOL:]


def pool_pattern(width):
    k, lane = iota((width, width), 0), iota((width, width), 1)
    hit = k // POOL == lane % (width // POOL)
    return jnp.where(hit, 1.0 / (POOL * POOL), 0.0).astype(jnp.bfloat16)


def pooled_cells(blocks, pattern):
    channels = blocks[0][0].shape[0]
    pairs = [
        jnp.concatenate([rows[i], rows[i + 1]], 1)
        for rows in blocks
        for i in range(0, POOL, 2)
    ]
    spread = jnp.concatenate([pattern, pattern], 0)
    parts = jnp.dot(jnp.concatenate(pairs, 0), spread, preferred_element_type=jnp.float32)
    results = []
    for k in range(len(blocks)):
        average = None
        for i in range(POOL // 2):
            place = (k * (POOL // 2) + i) * channels
            part = parts[place : place + channels]
            average = part if average is None else average + part
        mean = jnp.mean(average * average, axis=0, keepdims=True)
        results.append(average * lax.rsqrt(mean + 1e-6))
    return results


def pack_rows(values, turn, lanes):
    group = lanes // PACK
    width = lanes.shape[1]
    result = None
    for j, value in enumerate(values):
        shift = (PACK * j + turn) % width
        if shift:
            value = pltpu.roll(value, shift, 1)
        result = value if result is None else jnp.where(group == j, value, result)
    return result


def send_kernel(counts, tissue, embeddings, send_ref, far_ref):
    _, depth, height, channels, width = embeddings.shape
    cells = width // POOL
    tiles = depth * height // POOL
    per_row = width // (2 * cells)
    zs = width // PACK
    rim_rows = depth // zs * height * channels
    pool_rows = tiles // per_row * channels

    def run(bricks, sems):
        count = counts[0]
        last = count - 1
        second = jnp.maximum(count - 2, 0)
        copies = {}
        for z in range(depth):
            for k, slot in enumerate((last, second)):
                copy = pltpu.make_async_copy(embeddings.at[slot, z], bricks.at[k, z], sems.at[k, z])
                copy.start()
                copies[k, z] = copy
        lanes = iota((channels, width), 1)
        pattern = pool_pattern(width)
        own_mark = tissue[last].astype(jnp.float32)
        has_two = (count >= 2).astype(jnp.float32)
        second_mark = tissue[second].astype(jnp.float32) * has_two
        row = iota((16, width), 0)
        flags = jnp.where(row == 0, own_mark, jnp.where(row == 1, second_mark, has_two))
        send_ref[rim_rows + pool_rows :, :] = flags.astype(jnp.bfloat16)
        far_ref[pool_rows:, :] = flags.astype(jnp.bfloat16)
        planes = per_row * POOL // height
        for group in range(depth // zs):
            for z in range(group * zs, group * zs + zs):
                copies[0, z].wait()
                copies[1, z].wait()
            for y in range(height):
                values = [bricks[0, group * zs + j, y] for j in range(zs)]
                place = (group * height + y) * channels
                send_ref[place : place + channels, :] = pack_rows(values, PACK, lanes)
            for block in range(group * zs // planes, (group + 1) * zs // planes):
                total = jnp.zeros((channels, width), jnp.float32)
                for part in range(per_row):
                    tile = block * per_row + part
                    z, y0 = tile // (height // POOL), tile % (height // POOL) * POOL
                    blocks = [[bricks[k, z, y0 + i] for i in range(POOL)] for k in range(2)]
                    for k, value in enumerate(pooled_cells(blocks, pattern)):
                        total = jnp.where(lanes // cells == 2 * part + 1 - k, value, total)
                total = total.astype(jnp.bfloat16)
                place = block * channels
                far_ref[place : place + channels, :] = total
                send_ref[rim_rows + place : rim_rows + place + channels, :] = total

    pl.run_scoped(
        run,
        pltpu.VMEM((2, depth, height, channels, width), jnp.bfloat16),
        pltpu.SemaphoreType.DMA((2, depth)),
    )


def fine_kernel(counts, tissue, embeddings, fine_ref, pooled, head):
    slots, depth, height, channels, width = embeddings.shape
    offsets = len(FINE_OFFSETS)
    cells = width // POOL
    tiles = depth * height // POOL
    zs = width // PACK
    bf16 = jnp.bfloat16

    def running(k):
        return (k < counts[0]) & (tissue[k] > 0)

    def run(bricks, shifted, fine, patterns, pairs, weights, sems, out_sems):
        def plane_copy(k, z):
            return pltpu.make_async_copy(embeddings.at[k, z], bricks.at[k, z], sems.at[k, z])

        def fine_copy(k):
            return pltpu.make_async_copy(fine.at[k], fine_ref.at[k], out_sems.at[k])

        for k in range(slots):

            @pl.when(running(k))
            def _():
                for z in range(depth):
                    plane_copy(k, z).start()

        for k in range(slots):

            @pl.when(jnp.logical_not(running(k)))
            def _():
                fine[k] = jnp.zeros((offsets, depth, height, width), bf16)
                fine_copy(k).start()

        write_patterns(patterns, pairs, channels)
        pooled[...] = jnp.zeros_like(pooled)
        lanes = iota((channels, width), 1)
        rows, columns = iota((POOL, width), 0), iota((POOL, width), 1)
        keys = mask_keys(height)

        def do_slot(slot, carry):
            before = jnp.maximum(slot - 1, 0)
            left_ok = (slot > 0) & (tissue[before] > 0)
            for k, (step_x, start, stop) in enumerate(keys):
                inside = columns >= jnp.where(left_ok, 0, step_x)
                inside = inside & (rows >= start) & (rows < stop)
                weights[k] = jnp.where(inside, 0.5, 0.0)

            def prior_of(k):
                ahead = jnp.maximum(k - 1, 0)
                return jnp.where(running(ahead), ahead, k)

            def shift_row(k, z, y):
                own, prior = bricks[k, z, y], bricks[prior_of(k), z, y]
                for i, step in enumerate(SHIFTS):
                    joined = jnp.where(lanes >= width - step, prior, own)
                    shifted[i, z, y] = pltpu.roll(joined, step, 1)

            def plane(z, steps, final):
                if final:
                    after, next_z = jnp.minimum(slot + 1, slots - 1), 0
                else:
                    after, next_z = slot, z + 1
                pattern = pool_pattern(width)
                todo = list(range(height))
                units = 0
                for half in range(height // POOL):
                    first = half * POOL
                    centres = [bricks[slot, z, first + i] for i in range(POOL)]
                    (value,) = pooled_cells([centres], pattern)
                    place = (z * (height // POOL) + half) * channels
                    place = pl.ds(place, channels)
                    keep = lanes // cells == slot + 2
                    pooled[place, :] = jnp.where(keep, value.astype(bf16), pooled[place, :])
                    centre = lambda y: centres[y - first]

                    def partner_of(index):
                        step_z, _, step_x = FINE_OFFSETS[index]
                        if step_x:
                            k = SHIFTS.index(step_x)
                            return lambda y: shifted[k, z - step_z, y]
                        return lambda y: bricks[slot, z - step_z, y]

                    def finish(index, value):
                        _, step_y, step_x = FINE_OFFSETS[index]
                        start, stop = valid_rows(step_y, height, first)
                        weight = weights[keys.index((step_x, start - first, stop - first))]
                        value = value * weight + weight
                        fine[slot, index, z, first : first + POOL] = value.astype(bf16)

                    singles, doubles = [], []
                    for index, (step_z, step_y, _) in enumerate(FINE_OFFSETS):
                        start, stop = valid_rows(step_y, height, first)
                        if start >= stop or (step_z and step_z not in steps):
                            blank = jnp.zeros((POOL, width), bf16)
                            fine[slot, index, z, first : first + POOL] = blank
                        elif step_y in FOLDED:
                            doubles.append(index)
                        else:
                            singles.append(index)
                    if len(doubles) % 2:
                        singles.append(doubles.pop())
                    jobs = [(index,) for index in singles]
                    jobs += [tuple(doubles[i : i + 2]) for i in range(0, len(doubles), 2)]
                    jobs.sort(key=lambda job: FINE_OFFSETS[job[0]][2])
                    for job in jobs:
                        step_ys = [FINE_OFFSETS[index][1] for index in job]
                        partners = [partner_of(index) for index in job]
                        if len(job) == 1:
                            values = [
                                affinity_of(
                                    step_ys[0], height, first, patterns, centre, partners[0]
                                )
                            ]
                        else:
                            values = two_affinities(
                                step_ys, height, first, pairs, centre, partners
                            )
                        for index, value in zip(job, values):
                            finish(index, value)
                        units += len(job)
                        while todo and units >= 2 * (height - len(todo) + 1):
                            shift_row(after, next_z, todo.pop(0))
                for y in todo:
                    shift_row(after, next_z, y)

            @pl.when(running(slot) & ((slot == 0) | jnp.logical_not(running(before))))
            def _():
                plane_copy(slot, 0).wait()
                for y in range(height):
                    shift_row(slot, 0, y)

            @pl.when(running(slot))
            def _():
                last = depth - 1
                follower = jnp.minimum(slot + 1, slots - 1)
                for low in range(0, depth, PLANES):
                    for z in range(low + 1, min(low + PLANES, last) + 1):
                        plane_copy(slot, z).wait()
                    if low + PLANES >= depth:

                        @pl.when((slot + 1 < slots) & running(follower))
                        def _():
                            plane_copy(follower, 0).wait()

                    for z in range(low, low + PLANES):
                        steps = [offset[0] for offset in FINE_OFFSETS if 0 < offset[0] <= z]
                        plane(z, steps, z == last)

                fine_copy(slot).start()

            return carry

        lax.fori_loop(0, slots, do_slot, 0)

        @pl.when(running(0))
        def _():
            for group in range(depth // zs):
                for y in range(height):
                    values = [bricks[0, group * zs + j, y] for j in range(zs)]
                    place = (group * height + y) * channels
                    head[place : place + channels, :] = pack_rows(values, 0, lanes)

        for k in range(slots):
            fine_copy(k).wait()

    pl.run_scoped(
        run,
        pltpu.VMEM((slots, depth, height, channels, width), bf16),
        pltpu.VMEM((len(SHIFTS), depth, height, channels, width), bf16),
        pltpu.VMEM((slots, offsets, depth, height, width), bf16),
        pltpu.VMEM((len(STARTS), POOL, POOL * channels // 2), bf16),
        pltpu.VMEM((len(STARTS) ** 2, 2 * POOL, POOL * channels // 2), bf16),
        pltpu.VMEM((len(mask_keys(height)), POOL, width), jnp.float32),
        pltpu.SemaphoreType.DMA((slots, depth)),
        pltpu.SemaphoreType.DMA((slots,)),
    )


def join_kernel(
    counts, tissue, near_ref, far_ref, pooled_ref, head_ref, fine_in, fine_out, coarse_ref
):
    slots, cells_total = coarse_ref.shape
    _, offsets_fine, depth, height, width = fine_in.shape
    zs = width // PACK
    groups = depth // zs
    cells = width // POOL
    tiles = depth * height // POOL
    channels = head_ref.shape[0] // (groups * height)
    per_row = width // (2 * cells)
    rim_rows = groups * height * channels
    pool_rows = tiles // per_row * channels

    inner = [index for index, offset in enumerate(FINE_OFFSETS) if offset[2] > 0]

    def run(fine, patch, rims, heads, turned, sums, sems):
        active = tissue[0] > 0
        fetch = pltpu.make_async_copy(fine_in.at[0], fine, sems.at[0])
        store = pltpu.make_async_copy(fine, fine_out.at[0], sems.at[1])
        rim_copy = pltpu.make_async_copy(near_ref.at[:rim_rows], rims, sems.at[2])
        head_copy = pltpu.make_async_copy(head_ref, heads, sems.at[3])

        @pl.when(active)
        def _():
            rim_copy.start()
            head_copy.start()
            fetch.start()

        lanes = iota((channels, width), 1)
        write_sums(sums, channels)
        near_flags = near_ref[rim_rows + pool_rows :, :].astype(jnp.float32)
        far_flags = far_ref[pool_rows:, :].astype(jnp.float32)
        near_mark, second_mark, has_two = near_flags[0:1], near_flags[1:2], near_flags[2:3]
        far_mark = jnp.where(has_two > 0, second_mark, far_flags[0:1])

        @pl.when(active)
        def _():
            def at(group, y):
                row = (group * height + y) * channels
                return slice(row, row + channels)

            rim_copy.wait()
            head_copy.wait()
            for y in range(height):
                values = [rims[at(group, y), :] for group in range(groups)]
                for k, (step_x, step_z) in enumerate(RIM_TURNS):
                    shift = (step_x + PACK * step_z - PACK) % width
                    held = None
                    for group in range(groups):
                        value = pltpu.roll(values[group], shift, 1)
                        fresh = value
                        if held is not None and step_z:
                            fresh = jnp.where(lanes < PACK * step_z, held, value)
                        turned[k, group, y] = fresh
                        held = value
            rows, columns = iota((height, width), 0), iota((height, width), 1)
            near_rows = jnp.broadcast_to(near_mark, (height, width)) > 0
            for k, index in enumerate(inner):
                step_z, step_y, step_x = FINE_OFFSETS[index]
                for group in range(groups):
                    if (group + 1) * zs <= step_z:
                        continue
                    if step_z >= zs:
                        turn, source = RIM_TURNS.index((step_x, 0)), group - step_z // zs
                    else:
                        turn, source = RIM_TURNS.index((step_x, step_z)), group
                    blank = jnp.zeros((channels // 4, width), jnp.bfloat16)
                    products = [
                        folded_product(heads[at(group, y), :], turned[turn, source, y - step_y], 2)
                        if 0 <= y - step_y < height
                        else blank
                        for y in range(height)
                    ]
                    score = jnp.dot(
                        sums[...],
                        jnp.concatenate(products, 0),
                        preferred_element_type=jnp.float32,
                    )
                    inside = near_rows
                    if step_y > 0:
                        inside = inside & (rows >= step_y)
                    if step_y < 0:
                        inside = inside & (rows < height + step_y)
                    value = jnp.where(inside, 0.5 * jnp.tanh(score) + 0.5, 0.0)
                    value = value.astype(jnp.bfloat16)
                    for j in range(zs):
                        z = group * zs + j
                        if z >= step_z:
                            moved = pltpu.roll(value, width - PACK * j, 1) if j else value
                            patch[k, z] = moved
            fetch.wait()
            for k, index in enumerate(inner):
                step_z, _, step_x = FINE_OFFSETS[index]
                for z in range(step_z, depth):
                    fine[index, z] = jnp.where(columns < step_x, patch[k, z], fine[index, z])
            store.start()

        out_x = iota((1, width), 1)
        mark = jnp.where(out_x < cells, far_mark, near_mark)
        for k in range(slots):
            own = jnp.where((k < counts[0]) & (tissue[k] > 0), 1.0, 0.0)
            mark = jnp.where(out_x >= (k + 2) * cells, own, mark)
        mark = jnp.where(out_x >= (slots + 2) * cells, 0.0, mark)
        offsets = (CO_NEAR, CO_FAR)
        scores = [[] for _ in offsets]
        for tile in range(tiles):
            block, part = tile // per_row, tile % per_row
            near_rows = slice(rim_rows + block * channels, rim_rows + (block + 1) * channels)
            far_rows = slice(block * channels, (block + 1) * channels)
            near = near_ref[near_rows, :]
            if part:
                near = pltpu.roll(near, width - 2 * part * cells, 1)
            far = pltpu.roll(far_ref[far_rows, :], width - (2 * part + 1) * cells, 1)
            far = jnp.where((has_two <= 0) & (lanes < cells), far.astype(jnp.float32), near.astype(jnp.float32))
            own = pooled_ref[tile * channels : (tile + 1) * channels, :].astype(jnp.float32)
            row = jnp.where(lanes < 2 * cells, far, own)
            for k, offset in enumerate(offsets):
                scores[k].append(jnp.sum(row * pltpu.roll(row, offset, 1), axis=0, keepdims=True))
        tables = []
        for k, offset in enumerate(offsets):
            score = jnp.concatenate(scores[k], 0)
            weight = mark * pltpu.roll(mark, offset, 1)
            value = 0.5 * jnp.tanh(score * (0.5 / math.sqrt(channels))) + 0.5
            tables.append(value * weight)
        table = jnp.concatenate(tables, 0).astype(jnp.bfloat16)
        count = table.shape[0]
        source, target = iota((width, cells_total), 0), iota((width, cells_total), 1)
        chosen = iota((count, cells_total), 0) == iota((count, cells_total), 1) // cells
        for k in range(slots):
            pick = jnp.where(source == (k + 2) * cells + target % cells, 1.0, 0.0)
            spread = jnp.dot(table, pick.astype(jnp.bfloat16), preferred_element_type=jnp.float32)
            line = jnp.sum(jnp.where(chosen, spread, 0.0), axis=0, keepdims=True)
            coarse_ref[k : k + 1, :] = line.astype(jnp.bfloat16)

        @pl.when(active)
        def _():
            store.wait()

    half = jnp.bfloat16
    pl.run_scoped(
        run,
        pltpu.VMEM((offsets_fine, depth, height, width), half),
        pltpu.VMEM((len(inner), depth, height, width), half),
        pltpu.VMEM((rim_rows, width), half),
        pltpu.VMEM((rim_rows, width), half),
        pltpu.VMEM((len(RIM_TURNS), groups, height, channels, width), half),
        pltpu.VMEM((height, height * channels // 4), half),
        pltpu.SemaphoreType.DMA((4,)),
    )


def body(embeddings, tissue, counts):
    slots, depth, height, channels, width = embeddings.shape
    offsets = len(FINE_OFFSETS)
    cells = width // POOL
    tiles = depth * height // POOL
    groups = depth // (width // PACK)
    rim_rows = groups * height * channels
    pool_rows = tiles * 2 * cells // width * channels
    smem = pl.BlockSpec(memory_space=pltpu.SMEM)
    anyspace = pl.BlockSpec(memory_space=pl.ANY)
    vmem = pl.BlockSpec(memory_space=pltpu.VMEM)
    half = jnp.bfloat16
    big = 40 * 1024 * 1024

    embeddings = pltpu.with_memory_space_constraint(embeddings, pltpu.HBM)
    tissue = pltpu.with_memory_space_constraint(tissue, pltpu.HBM)
    send, far = pl.pallas_call(
        send_kernel,
        out_shape=(
            pltpu.VMEM((rim_rows + pool_rows + 16, width), half),
            pltpu.VMEM((pool_rows + 16, width), half),
        ),
        in_specs=[smem, smem, anyspace],
        out_specs=(vmem, vmem),
        compiler_params=pltpu.CompilerParams(vmem_limit_bytes=big),
        name="send",
    )(counts, tissue, embeddings)

    axes = ("gz", "ba")
    devices = lax.axis_size(axes)
    near_in = lax.ppermute(send, axes, [(d, d + 1) for d in range(devices - 1)])
    far_in = lax.ppermute(far, axes, [(d, d + 2) for d in range(devices - 2)])

    fine, pooled, head = pl.pallas_call(
        fine_kernel,
        out_shape=(
            jax.ShapeDtypeStruct((slots, offsets, depth, height, width), half),
            pltpu.VMEM((tiles * channels, width), half),
            pltpu.VMEM((rim_rows, width), half),
        ),
        in_specs=[smem, smem, anyspace],
        out_specs=(anyspace, vmem, vmem),
        compiler_params=pltpu.CompilerParams(vmem_limit_bytes=big),
        cost_estimate=pl.CostEstimate(
            flops=20_000_000_000, bytes_accessed=20_000_000, transcendentals=0
        ),
        name="fine",
    )(counts, tissue, embeddings)

    near_in, far_in, pooled, head = (
        pltpu.with_memory_space_constraint(value, pltpu.VMEM)
        for value in (near_in, far_in, pooled, head)
    )
    return pl.pallas_call(
        join_kernel,
        out_shape=(
            jax.ShapeDtypeStruct(fine.shape, half),
            jax.ShapeDtypeStruct((slots, 2 * tiles * cells), half),
        ),
        in_specs=[smem, smem] + [vmem] * 4 + [anyspace],
        out_specs=(anyspace, vmem),
        input_output_aliases={6: 0},
        compiler_params=pltpu.CompilerParams(vmem_limit_bytes=big),
        name="join",
    )(counts, tissue, near_in, far_in, pooled, head, fine)


def solution(mesh):
    in_specs = (P(("gz", "ba"), None, None, None, None), P(("gz", "ba")), P(("gz", "ba")))
    out_specs = (P(("gz", "ba"), None, None, None, None), P(("gz", "ba"), None))
    return jax.shard_map(body, mesh=mesh, in_specs=in_specs, out_specs=out_specs, check_vma=False)
```

```python
import math

import jax
import jax.numpy as jnp
from jax import lax
from jax.experimental import pallas as pl
from jax.experimental.pallas import tpu as pltpu
from jax.sharding import PartitionSpec as P

CO_NEAR = 10
CO_FAR = 30
POOL = 8
PACK = 32

FINE_OFFSETS = (
    (0, 0, 1),
    (0, 0, 3),
    (0, 0, 9),
    (0, 0, 27),
    (0, 1, 0),
    (0, 3, 0),
    (0, 9, 0),
    (1, 0, 0),
    (2, 0, 0),
    (4, 0, 0),
    (0, 1, 1),
    (0, 3, 3),
    (0, 9, 9),
    (0, 9, 27),
    (0, -1, 1),
    (0, -3, 3),
    (0, -9, 9),
    (0, -9, 27),
    (1, 0, 3),
    (2, 0, 9),
    (4, 0, 27),
    (1, 1, 0),
    (2, 3, 0),
    (4, 9, 0),
    (1, 1, 1),
    (2, 3, 9),
)
SHIFTS = (1, 3, 9, 27)
STARTS = (0, 1, 3)
PLANES = 8
FOLDED = (0, 1, -1, 3, -3, 9, -9)
RIM_TURNS = ((1, 0), (3, 0), (9, 0), (27, 0), (3, 1), (1, 1), (9, 2))


def iota(shape, dim):
    return lax.broadcasted_iota(jnp.int32, shape, dim)


def write_patterns(ref, pair_ref, channels):
    _, rows, width = ref.shape
    scale = 0.5 / math.sqrt(channels)
    for k, start in enumerate(STARTS):
        hit = iota((rows, width), 1) // (channels // 2) + start == iota((rows, width), 0)
        ref[k] = jnp.where(hit, scale, 0.0).astype(jnp.bfloat16)
    row, column = iota((2 * rows, width), 0), iota((2 * rows, width), 1)
    place = column // (channels // 4)
    for i, low in enumerate(STARTS):
        for j, high in enumerate(STARTS):
            start = jnp.where(place < rows, low, high)
            hit = (place % rows + start == row % rows) & (place // rows == row // rows)
            pair_ref[i * len(STARTS) + j] = jnp.where(hit, scale, 0.0).astype(jnp.bfloat16)


def folded_product(left, right, levels):
    product = left * right
    for _ in range(levels):
        half = product.shape[0] // 2
        product = product[:half] + product[half:]
    return product


def valid_rows(step_y, height, first):
    start = max(first, step_y, 0)
    stop = min(first + POOL, height + min(step_y, 0))
    return start, stop


def stacked_products(step_y, height, first, levels, centre, partner):
    start, stop = valid_rows(step_y, height, first)
    products = [folded_product(centre(y), partner(y - step_y), levels) for y in range(start, stop)]
    blank = jnp.zeros_like(products[0])
    return products + [blank] * (POOL - len(products)), STARTS.index(start - first)


def mask_keys(height):
    keys = []
    for _, step_y, step_x in FINE_OFFSETS:
        for first in range(0, height, POOL):
            start, stop = valid_rows(step_y, height, first)
            key = (step_x, start - first, stop - first)
            if start < stop and key not in keys:
                keys.append(key)
    return keys


def affinity_of(step_y, height, first, patterns, centre, partner):
    products, start = stacked_products(step_y, height, first, 1, centre, partner)
    products = jnp.concatenate(products, 0)
    return jnp.tanh(jnp.dot(patterns[start], products, preferred_element_type=jnp.float32))


def write_sums(ref, channels):
    rows, width = ref.shape
    hit = iota((rows, width), 1) // (width // rows) == iota((rows, width), 0)
    ref[...] = jnp.where(hit, 0.5 / math.sqrt(channels), 0.0).astype(jnp.bfloat16)


def two_affinities(step_ys, height, first, patterns, centre, partners):
    products, starts = [], []
    for step_y, partner in zip(step_ys, partners):
        more, start = stacked_products(step_y, height, first, 2, centre, partner)
        products += more
        starts.append(start)
    pattern = patterns[starts[0] * len(STARTS) + starts[1]]
    products = jnp.concatenate(products, 0)
    value = jnp.tanh(jnp.dot(pattern, products, preferred_element_type=jnp.float32))
    return value[:POOL], value[POOL:]


def pool_pattern(width):
    k, lane = iota((width, width), 0), iota((width, width), 1)
    hit = k // POOL == lane % (width // POOL)
    return jnp.where(hit, 1.0 / (POOL * POOL), 0.0).astype(jnp.bfloat16)


def pooled_cells(blocks, pattern):
    channels = blocks[0][0].shape[0]
    pairs = [
        jnp.concatenate([rows[i] + rows[i + 1], rows[i + 2] + rows[i + 3]], 1)
        for rows in blocks
        for i in range(0, POOL, 4)
    ]
    spread = jnp.concatenate([pattern, pattern], 0)
    parts = jnp.dot(jnp.concatenate(pairs, 0), spread, preferred_element_type=jnp.float32)
    results = []
    for k in range(len(blocks)):
        average = None
        for i in range(POOL // 4):
            place = (k * (POOL // 4) + i) * channels
            part = parts[place : place + channels]
            average = part if average is None else average + part
        mean = jnp.mean(average * average, axis=0, keepdims=True)
        results.append(average * lax.rsqrt(mean + 1e-6))
    return results


def pack_rows(values, turn, lanes):
    group = lanes // PACK
    width = lanes.shape[1]
    result = None
    for j, value in enumerate(values):
        shift = (PACK * j + turn) % width
        if shift:
            value = pltpu.roll(value, shift, 1)
        result = value if result is None else jnp.where(group == j, value, result)
    return result


def send_kernel(counts, tissue, embeddings, send_ref, far_ref):
    _, depth, height, channels, width = embeddings.shape
    cells = width // POOL
    tiles = depth * height // POOL
    per_row = width // (2 * cells)
    zs = width // PACK
    rim_rows = depth // zs * height * channels
    pool_rows = tiles // per_row * channels

    def run(bricks, sems):
        count = counts[0]
        last = count - 1
        second = jnp.maximum(count - 2, 0)
        copies = {}
        for z in range(depth):
            for k, slot in enumerate((last, second)):
                copy = pltpu.make_async_copy(embeddings.at[slot, z], bricks.at[k, z], sems.at[k, z])
                copy.start()
                copies[k, z] = copy
        lanes = iota((channels, width), 1)
        pattern = pool_pattern(width)
        own_mark = tissue[last].astype(jnp.float32)
        has_two = (count >= 2).astype(jnp.float32)
        second_mark = tissue[second].astype(jnp.float32) * has_two
        row = iota((16, width), 0)
        flags = jnp.where(row == 0, own_mark, jnp.where(row == 1, second_mark, has_two))
        send_ref[rim_rows + pool_rows :, :] = flags.astype(jnp.bfloat16)
        far_ref[pool_rows:, :] = flags.astype(jnp.bfloat16)
        planes = per_row * POOL // height
        for group in range(depth // zs):
            for z in range(group * zs, group * zs + zs):
                copies[0, z].wait()
                copies[1, z].wait()
            for y in range(height):
                values = [bricks[0, group * zs + j, y] for j in range(zs)]
                place = (group * height + y) * channels
                send_ref[place : place + channels, :] = pack_rows(values, PACK, lanes)
            for block in range(group * zs // planes, (group + 1) * zs // planes):
                total = jnp.zeros((channels, width), jnp.float32)
                for part in range(per_row):
                    tile = block * per_row + part
                    z, y0 = tile // (height // POOL), tile % (height // POOL) * POOL
                    blocks = [[bricks[k, z, y0 + i] for i in range(POOL)] for k in range(2)]
                    for k, value in enumerate(pooled_cells(blocks, pattern)):
                        total = jnp.where(lanes // cells == 2 * part + 1 - k, value, total)
                total = total.astype(jnp.bfloat16)
                place = block * channels
                far_ref[place : place + channels, :] = total
                send_ref[rim_rows + place : rim_rows + place + channels, :] = total

    pl.run_scoped(
        run,
        pltpu.VMEM((2, depth, height, channels, width), jnp.bfloat16),
        pltpu.SemaphoreType.DMA((2, depth)),
    )


def fine_kernel(counts, tissue, embeddings, fine_ref, pooled, head):
    slots, depth, height, channels, width = embeddings.shape
    offsets = len(FINE_OFFSETS)
    cells = width // POOL
    tiles = depth * height // POOL
    zs = width // PACK
    bf16 = jnp.bfloat16

    def running(k):
        return (k < counts[0]) & (tissue[k] > 0)

    def run(bricks, shifted, fine, patterns, pairs, weights, sems, out_sems):
        def plane_copy(k, z):
            return pltpu.make_async_copy(embeddings.at[k, z], bricks.at[k, z], sems.at[k, z])

        def fine_copy(k):
            return pltpu.make_async_copy(fine.at[k], fine_ref.at[k], out_sems.at[k])

        for k in range(slots):

            @pl.when(running(k))
            def _():
                for z in range(depth):
                    plane_copy(k, z).start()

        for k in range(slots):

            @pl.when(jnp.logical_not(running(k)))
            def _():
                fine[k] = jnp.zeros((offsets, depth, height, width), bf16)
                fine_copy(k).start()

        write_patterns(patterns, pairs, channels)
        pooled[...] = jnp.zeros_like(pooled)
        lanes = iota((channels, width), 1)
        rows, columns = iota((POOL, width), 0), iota((POOL, width), 1)
        keys = mask_keys(height)

        def do_slot(slot, carry):
            before = jnp.maximum(slot - 1, 0)
            left_ok = (slot > 0) & (tissue[before] > 0)
            for k, (step_x, start, stop) in enumerate(keys):
                inside = columns >= jnp.where(left_ok, 0, step_x)
                inside = inside & (rows >= start) & (rows < stop)
                weights[k] = jnp.where(inside, 0.5, 0.0)

            def prior_of(k):
                ahead = jnp.maximum(k - 1, 0)
                return jnp.where(running(ahead), ahead, k)

            def shift_row(k, z, y):
                own, prior = bricks[k, z, y], bricks[prior_of(k), z, y]
                for i, step in enumerate(SHIFTS):
                    joined = jnp.where(lanes >= width - step, prior, own)
                    shifted[i, z, y] = pltpu.roll(joined, step, 1)

            def plane(z, steps, final):
                if final:
                    after, next_z = jnp.minimum(slot + 1, slots - 1), 0
                else:
                    after, next_z = slot, z + 1
                pattern = pool_pattern(width)
                todo = list(range(height))
                units = 0
                for half in range(height // POOL):
                    first = half * POOL
                    centres = [bricks[slot, z, first + i] for i in range(POOL)]
                    (value,) = pooled_cells([centres], pattern)
                    place = (z * (height // POOL) + half) * channels
                    place = pl.ds(place, channels)
                    keep = lanes // cells == slot + 2
                    pooled[place, :] = jnp.where(keep, value.astype(bf16), pooled[place, :])
                    centre = lambda y: centres[y - first]

                    def partner_of(index):
                        step_z, _, step_x = FINE_OFFSETS[index]
                        if step_x:
                            k = SHIFTS.index(step_x)
                            return lambda y: shifted[k, z - step_z, y]
                        return lambda y: bricks[slot, z - step_z, y]

                    def finish(index, value):
                        _, step_y, step_x = FINE_OFFSETS[index]
                        start, stop = valid_rows(step_y, height, first)
                        weight = weights[keys.index((step_x, start - first, stop - first))]
                        value = value * weight + weight
                        fine[slot, index, z, first : first + POOL] = value.astype(bf16)

                    singles, doubles = [], []
                    for index, (step_z, step_y, _) in enumerate(FINE_OFFSETS):
                        start, stop = valid_rows(step_y, height, first)
                        if start >= stop or (step_z and step_z not in steps):
                            blank = jnp.zeros((POOL, width), bf16)
                            fine[slot, index, z, first : first + POOL] = blank
                        elif step_y in FOLDED:
                            doubles.append(index)
                        else:
                            singles.append(index)
                    if len(doubles) % 2:
                        singles.append(doubles.pop())
                    jobs = [(index,) for index in singles]
                    jobs += [tuple(doubles[i : i + 2]) for i in range(0, len(doubles), 2)]
                    jobs.sort(key=lambda job: FINE_OFFSETS[job[0]][2])
                    for job in jobs:
                        step_ys = [FINE_OFFSETS[index][1] for index in job]
                        partners = [partner_of(index) for index in job]
                        if len(job) == 1:
                            values = [
                                affinity_of(
                                    step_ys[0], height, first, patterns, centre, partners[0]
                                )
                            ]
                        else:
                            values = two_affinities(
                                step_ys, height, first, pairs, centre, partners
                            )
                        for index, value in zip(job, values):
                            finish(index, value)
                        units += len(job)
                        while todo and units >= 2 * (height - len(todo) + 1):
                            shift_row(after, next_z, todo.pop(0))
                for y in todo:
                    shift_row(after, next_z, y)

            @pl.when(running(slot) & ((slot == 0) | jnp.logical_not(running(before))))
            def _():
                plane_copy(slot, 0).wait()
                for y in range(height):
                    shift_row(slot, 0, y)

            @pl.when(running(slot))
            def _():
                last = depth - 1
                follower = jnp.minimum(slot + 1, slots - 1)
                for low in range(0, depth, PLANES):
                    for z in range(low + 1, min(low + PLANES, last) + 1):
                        plane_copy(slot, z).wait()
                    if low + PLANES >= depth:

                        @pl.when((slot + 1 < slots) & running(follower))
                        def _():
                            plane_copy(follower, 0).wait()

                    for z in range(low, low + PLANES):
                        steps = [offset[0] for offset in FINE_OFFSETS if 0 < offset[0] <= z]
                        plane(z, steps, z == last)

                fine_copy(slot).start()

            return carry

        lax.fori_loop(0, slots, do_slot, 0)

        @pl.when(running(0))
        def _():
            for group in range(depth // zs):
                for y in range(height):
                    values = [bricks[0, group * zs + j, y] for j in range(zs)]
                    place = (group * height + y) * channels
                    head[place : place + channels, :] = pack_rows(values, 0, lanes)

        for k in range(slots):
            fine_copy(k).wait()

    pl.run_scoped(
        run,
        pltpu.VMEM((slots, depth, height, channels, width), bf16),
        pltpu.VMEM((len(SHIFTS), depth, height, channels, width), bf16),
        pltpu.VMEM((slots, offsets, depth, height, width), bf16),
        pltpu.VMEM((len(STARTS), POOL, POOL * channels // 2), bf16),
        pltpu.VMEM((len(STARTS) ** 2, 2 * POOL, POOL * channels // 2), bf16),
        pltpu.VMEM((len(mask_keys(height)), POOL, width), jnp.float32),
        pltpu.SemaphoreType.DMA((slots, depth)),
        pltpu.SemaphoreType.DMA((slots,)),
    )


def join_kernel(
    counts, tissue, near_ref, far_ref, pooled_ref, head_ref, fine_in, fine_out, coarse_ref
):
    slots, cells_total = coarse_ref.shape
    _, offsets_fine, depth, height, width = fine_in.shape
    zs = width // PACK
    groups = depth // zs
    cells = width // POOL
    tiles = depth * height // POOL
    channels = head_ref.shape[0] // (groups * height)
    per_row = width // (2 * cells)
    rim_rows = groups * height * channels
    pool_rows = tiles // per_row * channels

    inner = [index for index, offset in enumerate(FINE_OFFSETS) if offset[2] > 0]

    def run(fine, patch, rims, heads, turned, sums, sems):
        active = tissue[0] > 0
        fetch = pltpu.make_async_copy(fine_in.at[0], fine, sems.at[0])
        store = pltpu.make_async_copy(fine, fine_out.at[0], sems.at[1])
        rim_copy = pltpu.make_async_copy(near_ref.at[:rim_rows], rims, sems.at[2])
        head_copy = pltpu.make_async_copy(head_ref, heads, sems.at[3])

        @pl.when(active)
        def _():
            rim_copy.start()
            head_copy.start()
            fetch.start()

        lanes = iota((channels, width), 1)
        write_sums(sums, channels)
        near_flags = near_ref[rim_rows + pool_rows :, :].astype(jnp.float32)
        far_flags = far_ref[pool_rows:, :].astype(jnp.float32)
        near_mark, second_mark, has_two = near_flags[0:1], near_flags[1:2], near_flags[2:3]
        far_mark = jnp.where(has_two > 0, second_mark, far_flags[0:1])

        @pl.when(active)
        def _():
            def at(group, y):
                row = (group * height + y) * channels
                return slice(row, row + channels)

            rim_copy.wait()
            head_copy.wait()
            for y in range(height):
                values = [rims[at(group, y), :] for group in range(groups)]
                for k, (step_x, step_z) in enumerate(RIM_TURNS):
                    shift = (step_x + PACK * step_z - PACK) % width
                    held = None
                    for group in range(groups):
                        value = pltpu.roll(values[group], shift, 1)
                        fresh = value
                        if held is not None and step_z:
                            fresh = jnp.where(lanes < PACK * step_z, held, value)
                        turned[k, group, y] = fresh
                        held = value
            rows, columns = iota((height, width), 0), iota((height, width), 1)
            near_rows = jnp.broadcast_to(near_mark, (height, width)) > 0
            for k, index in enumerate(inner):
                step_z, step_y, step_x = FINE_OFFSETS[index]
                for group in range(groups):
                    if (group + 1) * zs <= step_z:
                        continue
                    if step_z >= zs:
                        turn, source = RIM_TURNS.index((step_x, 0)), group - step_z // zs
                    else:
                        turn, source = RIM_TURNS.index((step_x, step_z)), group
                    blank = jnp.zeros((channels // 4, width), jnp.bfloat16)
                    products = [
                        folded_product(heads[at(group, y), :], turned[turn, source, y - step_y], 2)
                        if 0 <= y - step_y < height
                        else blank
                        for y in range(height)
                    ]
                    score = jnp.dot(
                        sums[...],
                        jnp.concatenate(products, 0),
                        preferred_element_type=jnp.float32,
                    )
                    inside = near_rows
                    if step_y > 0:
                        inside = inside & (rows >= step_y)
                    if step_y < 0:
                        inside = inside & (rows < height + step_y)
                    value = jnp.where(inside, 0.5 * jnp.tanh(score) + 0.5, 0.0)
                    value = value.astype(jnp.bfloat16)
                    for j in range(zs):
                        z = group * zs + j
                        if z >= step_z:
                            moved = pltpu.roll(value, width - PACK * j, 1) if j else value
                            patch[k, z] = moved
            fetch.wait()
            for k, index in enumerate(inner):
                step_z, _, step_x = FINE_OFFSETS[index]
                for z in range(step_z, depth):
                    fine[index, z] = jnp.where(columns < step_x, patch[k, z], fine[index, z])
            store.start()

        out_x = iota((1, width), 1)
        mark = jnp.where(out_x < cells, far_mark, near_mark)
        for k in range(slots):
            own = jnp.where((k < counts[0]) & (tissue[k] > 0), 1.0, 0.0)
            mark = jnp.where(out_x >= (k + 2) * cells, own, mark)
        mark = jnp.where(out_x >= (slots + 2) * cells, 0.0, mark)
        offsets = (CO_NEAR, CO_FAR)
        scores = [[] for _ in offsets]
        for tile in range(tiles):
            block, part = tile // per_row, tile % per_row
            near_rows = slice(rim_rows + block * channels, rim_rows + (block + 1) * channels)
            far_rows = slice(block * channels, (block + 1) * channels)
            near = near_ref[near_rows, :]
            if part:
                near = pltpu.roll(near, width - 2 * part * cells, 1)
            far = pltpu.roll(far_ref[far_rows, :], width - (2 * part + 1) * cells, 1)
            far = jnp.where((has_two <= 0) & (lanes < cells), far.astype(jnp.float32), near.astype(jnp.float32))
            own = pooled_ref[tile * channels : (tile + 1) * channels, :].astype(jnp.float32)
            row = jnp.where(lanes < 2 * cells, far, own)
            for k, offset in enumerate(offsets):
                scores[k].append(jnp.sum(row * pltpu.roll(row, offset, 1), axis=0, keepdims=True))
        tables = []
        for k, offset in enumerate(offsets):
            score = jnp.concatenate(scores[k], 0)
            weight = mark * pltpu.roll(mark, offset, 1)
            value = 0.5 * jnp.tanh(score * (0.5 / math.sqrt(channels))) + 0.5
            tables.append(value * weight)
        table = jnp.concatenate(tables, 0).astype(jnp.bfloat16)
        count = table.shape[0]
        source, target = iota((width, cells_total), 0), iota((width, cells_total), 1)
        chosen = iota((count, cells_total), 0) == iota((count, cells_total), 1) // cells
        for k in range(slots):
            pick = jnp.where(source == (k + 2) * cells + target % cells, 1.0, 0.0)
            spread = jnp.dot(table, pick.astype(jnp.bfloat16), preferred_element_type=jnp.float32)
            line = jnp.sum(jnp.where(chosen, spread, 0.0), axis=0, keepdims=True)
            coarse_ref[k : k + 1, :] = line.astype(jnp.bfloat16)

        @pl.when(active)
        def _():
            store.wait()

    half = jnp.bfloat16
    pl.run_scoped(
        run,
        pltpu.VMEM((offsets_fine, depth, height, width), half),
        pltpu.VMEM((len(inner), depth, height, width), half),
        pltpu.VMEM((rim_rows, width), half),
        pltpu.VMEM((rim_rows, width), half),
        pltpu.VMEM((len(RIM_TURNS), groups, height, channels, width), half),
        pltpu.VMEM((height, height * channels // 4), half),
        pltpu.SemaphoreType.DMA((4,)),
    )


def body(embeddings, tissue, counts):
    slots, depth, height, channels, width = embeddings.shape
    offsets = len(FINE_OFFSETS)
    cells = width // POOL
    tiles = depth * height // POOL
    groups = depth // (width // PACK)
    rim_rows = groups * height * channels
    pool_rows = tiles * 2 * cells // width * channels
    smem = pl.BlockSpec(memory_space=pltpu.SMEM)
    anyspace = pl.BlockSpec(memory_space=pl.ANY)
    vmem = pl.BlockSpec(memory_space=pltpu.VMEM)
    half = jnp.bfloat16
    big = 40 * 1024 * 1024

    embeddings = pltpu.with_memory_space_constraint(embeddings, pltpu.HBM)
    tissue = pltpu.with_memory_space_constraint(tissue, pltpu.HBM)
    send, far = pl.pallas_call(
        send_kernel,
        out_shape=(
            pltpu.VMEM((rim_rows + pool_rows + 16, width), half),
            pltpu.VMEM((pool_rows + 16, width), half),
        ),
        in_specs=[smem, smem, anyspace],
        out_specs=(vmem, vmem),
        compiler_params=pltpu.CompilerParams(vmem_limit_bytes=big),
        name="send",
    )(counts, tissue, embeddings)

    axes = ("gz", "ba")
    devices = lax.axis_size(axes)
    near_in = lax.ppermute(send, axes, [(d, d + 1) for d in range(devices - 1)])
    far_in = lax.ppermute(far, axes, [(d, d + 2) for d in range(devices - 2)])

    fine, pooled, head = pl.pallas_call(
        fine_kernel,
        out_shape=(
            jax.ShapeDtypeStruct((slots, offsets, depth, height, width), half),
            pltpu.VMEM((tiles * channels, width), half),
            pltpu.VMEM((rim_rows, width), half),
        ),
        in_specs=[smem, smem, anyspace],
        out_specs=(anyspace, vmem, vmem),
        compiler_params=pltpu.CompilerParams(vmem_limit_bytes=big),
        cost_estimate=pl.CostEstimate(
            flops=20_000_000_000, bytes_accessed=20_000_000, transcendentals=0
        ),
        name="fine",
    )(counts, tissue, embeddings)

    near_in, far_in, pooled, head = (
        pltpu.with_memory_space_constraint(value, pltpu.VMEM)
        for value in (near_in, far_in, pooled, head)
    )
    return pl.pallas_call(
        join_kernel,
        out_shape=(
            jax.ShapeDtypeStruct(fine.shape, half),
            jax.ShapeDtypeStruct((slots, 2 * tiles * cells), half),
        ),
        in_specs=[smem, smem] + [vmem] * 4 + [anyspace],
        out_specs=(anyspace, vmem),
        input_output_aliases={6: 0},
        compiler_params=pltpu.CompilerParams(vmem_limit_bytes=big),
        name="join",
    )(counts, tissue, near_in, far_in, pooled, head, fine)


def solution(mesh):
    in_specs = (P(("gz", "ba"), None, None, None, None), P(("gz", "ba")), P(("gz", "ba")))
    out_specs = (P(("gz", "ba"), None, None, None, None), P(("gz", "ba"), None))
    return jax.shard_map(body, mesh=mesh, in_specs=in_specs, out_specs=out_specs, check_vma=False)
```

```python
import math

import jax
import jax.numpy as jnp
from jax import lax
from jax.experimental import pallas as pl
from jax.experimental.pallas import tpu as pltpu
from jax.sharding import PartitionSpec as P

CO_NEAR = 10
CO_FAR = 30
POOL = 8
PACK = 32

FINE_OFFSETS = (
    (0, 0, 1),
    (0, 0, 3),
    (0, 0, 9),
    (0, 0, 27),
    (0, 1, 0),
    (0, 3, 0),
    (0, 9, 0),
    (1, 0, 0),
    (2, 0, 0),
    (4, 0, 0),
    (0, 1, 1),
    (0, 3, 3),
    (0, 9, 9),
    (0, 9, 27),
    (0, -1, 1),
    (0, -3, 3),
    (0, -9, 9),
    (0, -9, 27),
    (1, 0, 3),
    (2, 0, 9),
    (4, 0, 27),
    (1, 1, 0),
    (2, 3, 0),
    (4, 9, 0),
    (1, 1, 1),
    (2, 3, 9),
)
SHIFTS = (1, 3, 9, 27)
STARTS = (0, 1, 3)
PLANES = 8
FOLDED = ()
RIM_TURNS = ((1, 0), (3, 0), (9, 0), (27, 0), (3, 1), (1, 1), (9, 2))


def iota(shape, dim):
    return lax.broadcasted_iota(jnp.int32, shape, dim)


def write_patterns(ref, pair_ref, channels):
    _, rows, width = ref.shape
    scale = 0.5 / math.sqrt(channels)
    for k, start in enumerate(STARTS):
        hit = iota((rows, width), 1) // (channels // 2) + start == iota((rows, width), 0)
        ref[k] = jnp.where(hit, scale, 0.0).astype(jnp.bfloat16)
    row, column = iota((2 * rows, width), 0), iota((2 * rows, width), 1)
    place = column // (channels // 4)
    for i, low in enumerate(STARTS):
        for j, high in enumerate(STARTS):
            start = jnp.where(place < rows, low, high)
            hit = (place % rows + start == row % rows) & (place // rows == row // rows)
            pair_ref[i * len(STARTS) + j] = jnp.where(hit, scale, 0.0).astype(jnp.bfloat16)


def folded_product(left, right, levels):
    product = left * right
    for _ in range(levels):
        half = product.shape[0] // 2
        product = product[:half] + product[half:]
    return product


def valid_rows(step_y, height, first):
    start = max(first, step_y, 0)
    stop = min(first + POOL, height + min(step_y, 0))
    return start, stop


def stacked_products(step_y, height, first, levels, centre, partner):
    start, stop = valid_rows(step_y, height, first)
    products = [folded_product(centre(y), partner(y - step_y), levels) for y in range(start, stop)]
    blank = jnp.zeros_like(products[0])
    return products + [blank] * (POOL - len(products)), STARTS.index(start - first)


def mask_keys(height):
    keys = []
    for _, step_y, step_x in FINE_OFFSETS:
        for first in range(0, height, POOL):
            start, stop = valid_rows(step_y, height, first)
            key = (step_x, start - first, stop - first)
            if start < stop and key not in keys:
                keys.append(key)
    return keys


def affinity_of(step_y, height, first, patterns, centre, partner):
    products, start = stacked_products(step_y, height, first, 1, centre, partner)
    products = jnp.concatenate(products, 0)
    return jnp.tanh(jnp.dot(patterns[start], products, preferred_element_type=jnp.float32))


def write_sums(ref, channels):
    rows, width = ref.shape
    hit = iota((rows, width), 1) // (width // rows) == iota((rows, width), 0)
    ref[...] = jnp.where(hit, 0.5 / math.sqrt(channels), 0.0).astype(jnp.bfloat16)


def two_affinities(step_ys, height, first, patterns, centre, partners):
    products, starts = [], []
    for step_y, partner in zip(step_ys, partners):
        more, start = stacked_products(step_y, height, first, 2, centre, partner)
        products += more
        starts.append(start)
    pattern = patterns[starts[0] * len(STARTS) + starts[1]]
    products = jnp.concatenate(products, 0)
    value = jnp.tanh(jnp.dot(pattern, products, preferred_element_type=jnp.float32))
    return value[:POOL], value[POOL:]


def pool_pattern(width):
    k, lane = iota((width, width), 0), iota((width, width), 1)
    hit = k // POOL == lane % (width // POOL)
    return jnp.where(hit, 1.0 / (POOL * POOL), 0.0).astype(jnp.bfloat16)


def pooled_cells(blocks, pattern):
    channels = blocks[0][0].shape[0]
    pairs = [
        jnp.concatenate([rows[i] + rows[i + 1], rows[i + 2] + rows[i + 3]], 1)
        for rows in blocks
        for i in range(0, POOL, 4)
    ]
    spread = jnp.concatenate([pattern, pattern], 0)
    parts = jnp.dot(jnp.concatenate(pairs, 0), spread, preferred_element_type=jnp.float32)
    results = []
    for k in range(len(blocks)):
        average = None
        for i in range(POOL // 4):
            place = (k * (POOL // 4) + i) * channels
            part = parts[place : place + channels]
            average = part if average is None else average + part
        mean = jnp.mean(average * average, axis=0, keepdims=True)
        results.append(average * lax.rsqrt(mean + 1e-6))
    return results


def pack_rows(values, turn, lanes):
    group = lanes // PACK
    width = lanes.shape[1]
    result = None
    for j, value in enumerate(values):
        shift = (PACK * j + turn) % width
        if shift:
            value = pltpu.roll(value, shift, 1)
        result = value if result is None else jnp.where(group == j, value, result)
    return result


def send_kernel(counts, tissue, embeddings, send_ref, far_ref):
    _, depth, height, channels, width = embeddings.shape
    cells = width // POOL
    tiles = depth * height // POOL
    per_row = width // (2 * cells)
    zs = width // PACK
    rim_rows = depth // zs * height * channels
    pool_rows = tiles // per_row * channels

    def run(bricks, sems):
        count = counts[0]
        last = count - 1
        second = jnp.maximum(count - 2, 0)
        copies = {}
        for z in range(depth):
            for k, slot in enumerate((last, second)):
                copy = pltpu.make_async_copy(embeddings.at[slot, z], bricks.at[k, z], sems.at[k, z])
                copy.start()
                copies[k, z] = copy
        lanes = iota((channels, width), 1)
        pattern = pool_pattern(width)
        own_mark = tissue[last].astype(jnp.float32)
        has_two = (count >= 2).astype(jnp.float32)
        second_mark = tissue[second].astype(jnp.float32) * has_two
        row = iota((16, width), 0)
        flags = jnp.where(row == 0, own_mark, jnp.where(row == 1, second_mark, has_two))
        send_ref[rim_rows + pool_rows :, :] = flags.astype(jnp.bfloat16)
        far_ref[pool_rows:, :] = flags.astype(jnp.bfloat16)
        planes = per_row * POOL // height
        for group in range(depth // zs):
            for z in range(group * zs, group * zs + zs):
                copies[0, z].wait()
                copies[1, z].wait()
            for y in range(height):
                values = [bricks[0, group * zs + j, y] for j in range(zs)]
                place = (group * height + y) * channels
                send_ref[place : place + channels, :] = pack_rows(values, PACK, lanes)
            for block in range(group * zs // planes, (group + 1) * zs // planes):
                total = jnp.zeros((channels, width), jnp.float32)
                for part in range(per_row):
                    tile = block * per_row + part
                    z, y0 = tile // (height // POOL), tile % (height // POOL) * POOL
                    blocks = [[bricks[k, z, y0 + i] for i in range(POOL)] for k in range(2)]
                    for k, value in enumerate(pooled_cells(blocks, pattern)):
                        total = jnp.where(lanes // cells == 2 * part + 1 - k, value, total)
                total = total.astype(jnp.bfloat16)
                place = block * channels
                far_ref[place : place + channels, :] = total
                send_ref[rim_rows + place : rim_rows + place + channels, :] = total

    pl.run_scoped(
        run,
        pltpu.VMEM((2, depth, height, channels, width), jnp.bfloat16),
        pltpu.SemaphoreType.DMA((2, depth)),
    )


def fine_kernel(counts, tissue, embeddings, fine_ref, pooled, head):
    slots, depth, height, channels, width = embeddings.shape
    offsets = len(FINE_OFFSETS)
    cells = width // POOL
    tiles = depth * height // POOL
    zs = width // PACK
    bf16 = jnp.bfloat16

    def running(k):
        return (k < counts[0]) & (tissue[k] > 0)

    def run(bricks, shifted, fine, patterns, pairs, weights, sems, out_sems):
        def plane_copy(k, z):
            return pltpu.make_async_copy(embeddings.at[k, z], bricks.at[k, z], sems.at[k, z])

        def fine_copy(k):
            return pltpu.make_async_copy(fine.at[k], fine_ref.at[k], out_sems.at[k])

        for k in range(slots):

            @pl.when(running(k))
            def _():
                for z in range(depth):
                    plane_copy(k, z).start()

        for k in range(slots):

            @pl.when(jnp.logical_not(running(k)))
            def _():
                fine[k] = jnp.zeros((offsets, depth, height, width), bf16)
                fine_copy(k).start()

        write_patterns(patterns, pairs, channels)
        pooled[...] = jnp.zeros_like(pooled)
        lanes = iota((channels, width), 1)
        rows, columns = iota((POOL, width), 0), iota((POOL, width), 1)
        keys = mask_keys(height)

        def do_slot(slot, carry):
            before = jnp.maximum(slot - 1, 0)
            left_ok = (slot > 0) & (tissue[before] > 0)
            for k, (step_x, start, stop) in enumerate(keys):
                inside = columns >= jnp.where(left_ok, 0, step_x)
                inside = inside & (rows >= start) & (rows < stop)
                weights[k] = jnp.where(inside, 0.5, 0.0)

            def prior_of(k):
                ahead = jnp.maximum(k - 1, 0)
                return jnp.where(running(ahead), ahead, k)

            def shift_row(k, z, y):
                own, prior = bricks[k, z, y], bricks[prior_of(k), z, y]
                for i, step in enumerate(SHIFTS):
                    joined = jnp.where(lanes >= width - step, prior, own)
                    shifted[i, z, y] = pltpu.roll(joined, step, 1)

            def plane(z, steps, final):
                if final:
                    after, next_z = jnp.minimum(slot + 1, slots - 1), 0
                else:
                    after, next_z = slot, z + 1
                pattern = pool_pattern(width)
                todo = list(range(height))
                units = 0
                for half in range(height // POOL):
                    first = half * POOL
                    centres = [bricks[slot, z, first + i] for i in range(POOL)]
                    (value,) = pooled_cells([centres], pattern)
                    place = (z * (height // POOL) + half) * channels
                    place = pl.ds(place, channels)
                    keep = lanes // cells == slot + 2
                    pooled[place, :] = jnp.where(keep, value.astype(bf16), pooled[place, :])
                    centre = lambda y: centres[y - first]

                    def partner_of(index):
                        step_z, _, step_x = FINE_OFFSETS[index]
                        if step_x:
                            k = SHIFTS.index(step_x)
                            return lambda y: shifted[k, z - step_z, y]
                        return lambda y: bricks[slot, z - step_z, y]

                    def finish(index, value):
                        _, step_y, step_x = FINE_OFFSETS[index]
                        start, stop = valid_rows(step_y, height, first)
                        weight = weights[keys.index((step_x, start - first, stop - first))]
                        value = value * weight + weight
                        fine[slot, index, z, first : first + POOL] = value.astype(bf16)

                    singles, doubles = [], []
                    for index, (step_z, step_y, _) in enumerate(FINE_OFFSETS):
                        start, stop = valid_rows(step_y, height, first)
                        if start >= stop or (step_z and step_z not in steps):
                            blank = jnp.zeros((POOL, width), bf16)
                            fine[slot, index, z, first : first + POOL] = blank
                        elif step_y in FOLDED:
                            doubles.append(index)
                        else:
                            singles.append(index)
                    if len(doubles) % 2:
                        singles.append(doubles.pop())
                    jobs = [(index,) for index in singles]
                    jobs += [tuple(doubles[i : i + 2]) for i in range(0, len(doubles), 2)]
                    for job in jobs:
                        step_ys = [FINE_OFFSETS[index][1] for index in job]
                        partners = [partner_of(index) for index in job]
                        if len(job) == 1:
                            values = [
                                affinity_of(
                                    step_ys[0], height, first, patterns, centre, partners[0]
                                )
                            ]
                        else:
                            values = two_affinities(
                                step_ys, height, first, pairs, centre, partners
                            )
                        for index, value in zip(job, values):
                            finish(index, value)
                        units += len(job)
                        while todo and units >= 2 * (height - len(todo) + 1):
                            shift_row(after, next_z, todo.pop(0))
                for y in todo:
                    shift_row(after, next_z, y)

            @pl.when(running(slot) & ((slot == 0) | jnp.logical_not(running(before))))
            def _():
                plane_copy(slot, 0).wait()
                for y in range(height):
                    shift_row(slot, 0, y)

            @pl.when(running(slot))
            def _():
                last = depth - 1
                follower = jnp.minimum(slot + 1, slots - 1)
                for low in range(0, depth, PLANES):
                    for z in range(low + 1, min(low + PLANES, last) + 1):
                        plane_copy(slot, z).wait()
                    if low + PLANES >= depth:

                        @pl.when((slot + 1 < slots) & running(follower))
                        def _():
                            plane_copy(follower, 0).wait()

                    for z in range(low, low + PLANES):
                        steps = [offset[0] for offset in FINE_OFFSETS if 0 < offset[0] <= z]
                        plane(z, steps, z == last)

                fine_copy(slot).start()

            return carry

        lax.fori_loop(0, slots, do_slot, 0)

        @pl.when(running(0))
        def _():
            for group in range(depth // zs):
                for y in range(height):
                    values = [bricks[0, group * zs + j, y] for j in range(zs)]
                    place = (group * height + y) * channels
                    head[place : place + channels, :] = pack_rows(values, 0, lanes)

        for k in range(slots):
            fine_copy(k).wait()

    pl.run_scoped(
        run,
        pltpu.VMEM((slots, depth, height, channels, width), bf16),
        pltpu.VMEM((len(SHIFTS), depth, height, channels, width), bf16),
        pltpu.VMEM((slots, offsets, depth, height, width), bf16),
        pltpu.VMEM((len(STARTS), POOL, POOL * channels // 2), bf16),
        pltpu.VMEM((len(STARTS) ** 2, 2 * POOL, POOL * channels // 2), bf16),
        pltpu.VMEM((len(mask_keys(height)), POOL, width), jnp.float32),
        pltpu.SemaphoreType.DMA((slots, depth)),
        pltpu.SemaphoreType.DMA((slots,)),
    )


def join_kernel(
    counts, tissue, near_ref, far_ref, pooled_ref, head_ref, fine_in, fine_out, coarse_ref
):
    slots, cells_total = coarse_ref.shape
    _, offsets_fine, depth, height, width = fine_in.shape
    zs = width // PACK
    groups = depth // zs
    cells = width // POOL
    tiles = depth * height // POOL
    channels = head_ref.shape[0] // (groups * height)
    per_row = width // (2 * cells)
    rim_rows = groups * height * channels
    pool_rows = tiles // per_row * channels

    inner = [index for index, offset in enumerate(FINE_OFFSETS) if offset[2] > 0]

    def run(fine, patch, rims, heads, turned, sums, sems):
        active = tissue[0] > 0
        fetch = pltpu.make_async_copy(fine_in.at[0], fine, sems.at[0])
        store = pltpu.make_async_copy(fine, fine_out.at[0], sems.at[1])
        rim_copy = pltpu.make_async_copy(near_ref.at[:rim_rows], rims, sems.at[2])
        head_copy = pltpu.make_async_copy(head_ref, heads, sems.at[3])

        @pl.when(active)
        def _():
            rim_copy.start()
            head_copy.start()
            fetch.start()

        lanes = iota((channels, width), 1)
        write_sums(sums, channels)
        near_flags = near_ref[rim_rows + pool_rows :, :].astype(jnp.float32)
        far_flags = far_ref[pool_rows:, :].astype(jnp.float32)
        near_mark, second_mark, has_two = near_flags[0:1], near_flags[1:2], near_flags[2:3]
        far_mark = jnp.where(has_two > 0, second_mark, far_flags[0:1])

        @pl.when(active)
        def _():
            def at(group, y):
                row = (group * height + y) * channels
                return slice(row, row + channels)

            rim_copy.wait()
            head_copy.wait()
            for y in range(height):
                values = [rims[at(group, y), :] for group in range(groups)]
                for k, (step_x, step_z) in enumerate(RIM_TURNS):
                    shift = (step_x + PACK * step_z - PACK) % width
                    held = None
                    for group in range(groups):
                        value = pltpu.roll(values[group], shift, 1)
                        fresh = value
                        if held is not None and step_z:
                            fresh = jnp.where(lanes < PACK * step_z, held, value)
                        turned[k, group, y] = fresh
                        held = value
            rows, columns = iota((height, width), 0), iota((height, width), 1)
            near_rows = jnp.broadcast_to(near_mark, (height, width)) > 0
            for k, index in enumerate(inner):
                step_z, step_y, step_x = FINE_OFFSETS[index]
                for group in range(groups):
                    if (group + 1) * zs <= step_z:
                        continue
                    if step_z >= zs:
                        turn, source = RIM_TURNS.index((step_x, 0)), group - step_z // zs
                    else:
                        turn, source = RIM_TURNS.index((step_x, step_z)), group
                    blank = jnp.zeros((channels // 4, width), jnp.bfloat16)
                    products = [
                        folded_product(heads[at(group, y), :], turned[turn, source, y - step_y], 2)
                        if 0 <= y - step_y < height
                        else blank
                        for y in range(height)
                    ]
                    score = jnp.dot(
                        sums[...],
                        jnp.concatenate(products, 0),
                        preferred_element_type=jnp.float32,
                    )
                    inside = near_rows
                    if step_y > 0:
                        inside = inside & (rows >= step_y)
                    if step_y < 0:
                        inside = inside & (rows < height + step_y)
                    value = jnp.where(inside, 0.5 * jnp.tanh(score) + 0.5, 0.0)
                    value = value.astype(jnp.bfloat16)
                    for j in range(zs):
                        z = group * zs + j
                        if z >= step_z:
                            moved = pltpu.roll(value, width - PACK * j, 1) if j else value
                            patch[k, z] = moved
            fetch.wait()
            for k, index in enumerate(inner):
                step_z, _, step_x = FINE_OFFSETS[index]
                for z in range(step_z, depth):
                    fine[index, z] = jnp.where(columns < step_x, patch[k, z], fine[index, z])
            store.start()

        out_x = iota((1, width), 1)
        mark = jnp.where(out_x < cells, far_mark, near_mark)
        for k in range(slots):
            own = jnp.where((k < counts[0]) & (tissue[k] > 0), 1.0, 0.0)
            mark = jnp.where(out_x >= (k + 2) * cells, own, mark)
        mark = jnp.where(out_x >= (slots + 2) * cells, 0.0, mark)
        offsets = (CO_NEAR, CO_FAR)
        scores = [[] for _ in offsets]
        for tile in range(tiles):
            block, part = tile // per_row, tile % per_row
            near_rows = slice(rim_rows + block * channels, rim_rows + (block + 1) * channels)
            far_rows = slice(block * channels, (block + 1) * channels)
            near = near_ref[near_rows, :]
            if part:
                near = pltpu.roll(near, width - 2 * part * cells, 1)
            far = pltpu.roll(far_ref[far_rows, :], width - (2 * part + 1) * cells, 1)
            far = jnp.where((has_two <= 0) & (lanes < cells), far.astype(jnp.float32), near.astype(jnp.float32))
            own = pooled_ref[tile * channels : (tile + 1) * channels, :].astype(jnp.float32)
            row = jnp.where(lanes < 2 * cells, far, own)
            for k, offset in enumerate(offsets):
                scores[k].append(jnp.sum(row * pltpu.roll(row, offset, 1), axis=0, keepdims=True))
        tables = []
        for k, offset in enumerate(offsets):
            score = jnp.concatenate(scores[k], 0)
            weight = mark * pltpu.roll(mark, offset, 1)
            value = 0.5 * jnp.tanh(score * (0.5 / math.sqrt(channels))) + 0.5
            tables.append(value * weight)
        table = jnp.concatenate(tables, 0).astype(jnp.bfloat16)
        count = table.shape[0]
        source, target = iota((width, cells_total), 0), iota((width, cells_total), 1)
        chosen = iota((count, cells_total), 0) == iota((count, cells_total), 1) // cells
        for k in range(slots):
            pick = jnp.where(source == (k + 2) * cells + target % cells, 1.0, 0.0)
            spread = jnp.dot(table, pick.astype(jnp.bfloat16), preferred_element_type=jnp.float32)
            line = jnp.sum(jnp.where(chosen, spread, 0.0), axis=0, keepdims=True)
            coarse_ref[k : k + 1, :] = line.astype(jnp.bfloat16)

        @pl.when(active)
        def _():
            store.wait()

    half = jnp.bfloat16
    pl.run_scoped(
        run,
        pltpu.VMEM((offsets_fine, depth, height, width), half),
        pltpu.VMEM((len(inner), depth, height, width), half),
        pltpu.VMEM((rim_rows, width), half),
        pltpu.VMEM((rim_rows, width), half),
        pltpu.VMEM((len(RIM_TURNS), groups, height, channels, width), half),
        pltpu.VMEM((height, height * channels // 4), half),
        pltpu.SemaphoreType.DMA((4,)),
    )


def body(embeddings, tissue, counts):
    slots, depth, height, channels, width = embeddings.shape
    offsets = len(FINE_OFFSETS)
    cells = width // POOL
    tiles = depth * height // POOL
    groups = depth // (width // PACK)
    rim_rows = groups * height * channels
    pool_rows = tiles * 2 * cells // width * channels
    smem = pl.BlockSpec(memory_space=pltpu.SMEM)
    anyspace = pl.BlockSpec(memory_space=pl.ANY)
    vmem = pl.BlockSpec(memory_space=pltpu.VMEM)
    half = jnp.bfloat16
    big = 40 * 1024 * 1024

    embeddings = pltpu.with_memory_space_constraint(embeddings, pltpu.HBM)
    tissue = pltpu.with_memory_space_constraint(tissue, pltpu.HBM)
    send, far = pl.pallas_call(
        send_kernel,
        out_shape=(
            pltpu.VMEM((rim_rows + pool_rows + 16, width), half),
            pltpu.VMEM((pool_rows + 16, width), half),
        ),
        in_specs=[smem, smem, anyspace],
        out_specs=(vmem, vmem),
        compiler_params=pltpu.CompilerParams(vmem_limit_bytes=big),
        name="send",
    )(counts, tissue, embeddings)

    axes = ("gz", "ba")
    devices = lax.axis_size(axes)
    near_in = lax.ppermute(send, axes, [(d, d + 1) for d in range(devices - 1)])
    far_in = lax.ppermute(far, axes, [(d, d + 2) for d in range(devices - 2)])

    fine, pooled, head = pl.pallas_call(
        fine_kernel,
        out_shape=(
            jax.ShapeDtypeStruct((slots, offsets, depth, height, width), half),
            pltpu.VMEM((tiles * channels, width), half),
            pltpu.VMEM((rim_rows, width), half),
        ),
        in_specs=[smem, smem, anyspace],
        out_specs=(anyspace, vmem, vmem),
        compiler_params=pltpu.CompilerParams(vmem_limit_bytes=big),
        cost_estimate=pl.CostEstimate(
            flops=20_000_000_000, bytes_accessed=20_000_000, transcendentals=0
        ),
        name="fine",
    )(counts, tissue, embeddings)

    near_in, far_in, pooled, head = (
        pltpu.with_memory_space_constraint(value, pltpu.VMEM)
        for value in (near_in, far_in, pooled, head)
    )
    return pl.pallas_call(
        join_kernel,
        out_shape=(
            jax.ShapeDtypeStruct(fine.shape, half),
            jax.ShapeDtypeStruct((slots, 2 * tiles * cells), half),
        ),
        in_specs=[smem, smem] + [vmem] * 4 + [anyspace],
        out_specs=(anyspace, vmem),
        input_output_aliases={6: 0},
        compiler_params=pltpu.CompilerParams(vmem_limit_bytes=big),
        name="join",
    )(counts, tissue, near_in, far_in, pooled, head, fine)


def solution(mesh):
    in_specs = (P(("gz", "ba"), None, None, None, None), P(("gz", "ba")), P(("gz", "ba")))
    out_specs = (P(("gz", "ba"), None, None, None, None), P(("gz", "ba"), None))
    return jax.shard_map(body, mesh=mesh, in_specs=in_specs, out_specs=out_specs, check_vma=False)
```
